512 devices in a mesh: lat: 8 (over x, z_hi), lon: 64 (over y, z_lo, core).
Axes of the slice: x: 4, y: 8, z: 8 (z_hi: 2, z_lo: 4; z = z_hi * 4 + z_lo), core: 2. Of those that a mesh axis runs over, the one named last changes fastest.
Arguments:
- queries: bfloat16 [96, 1024, 512], P('lat', 'lon'), may hold values from -6 to 6
- keys: bfloat16 [96, 1024, 512], P('lat', 'lon'), may hold values from -6 to 6
- values: bfloat16 [96, 1024, 512], P('lat', 'lon'), may hold values from -16 to 16
- upstream: bfloat16 [96, 1024, 1024], P('lat', 'lon'), may hold values from -6 to 6
- out_weight: bfloat16 [512, 1024], replicated, may hold values from -0.25 to 0.25
Outputs:
- grad_queries: bfloat16 [96, 1024, 512], P('lat', 'lon')
- grad_keys: bfloat16 [96, 1024, 512], P('lat', 'lon')
- grad_values: bfloat16 [96, 1024, 512], P('lat', 'lon')
- grad_weight: float32 [512, 1024], P('lon')
The draws below stay inside these ranges and needn't reach their ends.
All inputs are finite; a program needn't handle non-finite values.
Results may differ from the reference program's by a relative error of at most 0.035.
Values may be sent and summed in bfloat16 or wider, within the bound.
No kernel may reach another device: no remote copies, remote signals or barrier semaphores. Data moves between devices by JAX's collectives and lax.ppermute only.
A program may use at most 64 MiB of HBM per device.

```python
import jax
import jax.numpy as jnp
from jax import lax

HEADS = 8
HEAD_DIM = 64
D = 1024
RADIUS = 6
NLAT = 96
NLON = 1024
INNER = 512


def drawn_pair(key):
    seeded = jax.random.fold_in(key, 4242)
    query_key, key_key = jax.random.split(seeded, 2)
    grid_shape = (NLAT, NLON, INNER)
    query_base = jnp.clip(jax.random.normal(query_key, grid_shape, jnp.float32), -4.0, 4.0)
    key_base = jnp.clip(jax.random.normal(key_key, grid_shape, jnp.float32), -4.0, 4.0)
    return (query_base, key_base)


def draw_queries(key, part):
    return drawn_pair(key)[0].astype(jnp.bfloat16)


def draw_keys(key, part):
    return drawn_pair(key)[1].astype(jnp.bfloat16)


def strengthened(drawn, stream_key, source, target, parts, factor):
    def block_of(position):
        return (jnp.arange(drawn.shape[position]) // (drawn.shape[position] // parts)).reshape((-1,) + (1,) * (drawn.ndim - 1 - position))

    one_side = jax.random.permutation(stream_key, parts)[block_of(target)]
    other_side = (block_of(target) + parts // 2) % parts
    return jnp.where((block_of(source) == one_side) | (block_of(source) == other_side), factor * drawn, drawn)


def level_of(rng, extent, cuts, low, top_value):
    factor_of = 1.0
    for position, blocks in cuts:
        heights = jax.random.uniform(jax.random.fold_in(jax.random.fold_in(rng, 6), position), (blocks,), jnp.float32, low / len(cuts), top_value / len(cuts))
        factor_of = factor_of * jnp.repeat(jnp.exp(heights), extent[position] // blocks).reshape((-1,) + (1,) * (len(extent) - 1 - position))
    return factor_of


def noise(stream_key, shape, scale, most, pieces=(), held_as=jnp.bfloat16):
    result = scale * jax.random.normal(stream_key, shape, jnp.float32)
    if pieces:
        result = result * level_of(stream_key, shape, pieces, -0.22, 0.18)
    return jnp.clip(result, -most, most).astype(held_as)


def heavy_noise(own_key, extent, scale, limit, cuts, heavy, kind=jnp.bfloat16):
    array = scale * jax.random.normal(own_key, extent, jnp.float32)
    if cuts:
        array = array * level_of(own_key, extent, cuts, -0.22, 0.18)
    return jnp.clip(strengthened(array, jax.random.fold_in(own_key, 3), *heavy), -limit, limit).astype(kind)


def setup_inputs(seed: int = 0) -> dict:
    key_list = jax.random.split(jax.random.key(seed), 6)
    return {
        "queries": draw_queries(jax.random.fold_in(key_list[5], 71), 0),
        "keys": draw_keys(jax.random.fold_in(key_list[5], 71), 0),
        "values": heavy_noise(key_list[2], (NLAT, NLON, INNER), 1.0, 16.0, ((0, 8), (1, 64)), (1, 2, 64, 4.0)),
        "upstream": noise(key_list[3], (NLAT, NLON, D), 1.0, 6.0, ((0, 8), (1, 64))),
        "out_weight": noise(key_list[4], (INNER, D), INNER ** -0.5, 0.25),
    }


def pad_grid(grid):
    wrapped = jnp.concatenate([grid[:, NLON - RADIUS:], grid, grid[:, :RADIUS]], axis=1)
    return jnp.pad(wrapped, ((RADIUS, RADIUS), (0, 0), (0, 0)))


def window_of(padded, lat_row):
    span = 2 * RADIUS + 1
    block = lax.dynamic_slice_in_dim(padded, lat_row, span, 0)
    return jnp.stack([block[:, offset:offset + NLON] for offset in range(span)], axis=1)


def split_heads(window):
    span = 2 * RADIUS + 1
    return window.astype(jnp.float32).reshape(span, span, NLON, HEADS, HEAD_DIM)


def rows_inside(lat_row):
    span = 2 * RADIUS + 1
    global_row = lat_row + jnp.arange(span, dtype=jnp.int32) - RADIUS
    inside = (global_row >= 0) & (global_row < NLAT)
    return inside[:, None, None, None]


def reference(queries, keys, values, upstream, out_weight):
    score_scale = HEAD_DIM ** -0.5
    upstream_flat = upstream.reshape(NLAT * NLON, D)
    grad_attended = jnp.dot(upstream_flat, out_weight.T, preferred_element_type=jnp.float32).astype(jnp.bfloat16)
    grad_attended = grad_attended.reshape(NLAT, NLON, INNER)
    keys_pad = pad_grid(keys)
    values_pad = pad_grid(values)

    def forward_row(lat_row):
        query_row = lax.dynamic_index_in_dim(queries, lat_row, 0, keepdims=False)
        query_row = query_row.astype(jnp.float32).reshape(NLON, HEADS, HEAD_DIM)
        grad_row = lax.dynamic_index_in_dim(grad_attended, lat_row, 0, keepdims=False)
        grad_row = grad_row.astype(jnp.float32).reshape(NLON, HEADS, HEAD_DIM)
        key_window = split_heads(window_of(keys_pad, lat_row))
        value_window = split_heads(window_of(values_pad, lat_row))
        inside = rows_inside(lat_row)
        scores = jnp.einsum('nhd,abnhd->abnh', query_row, key_window) * score_scale
        row_max = jnp.max(jnp.where(inside, scores, -jnp.inf), axis=(0, 1))
        raw_weights = jnp.where(inside, jnp.exp(scores - row_max), 0.0)
        totals = jnp.sum(raw_weights, axis=(0, 1))
        probs = raw_weights / totals
        log_norm = row_max + jnp.log(totals)
        probs_low = lax.optimization_barrier(probs.astype(jnp.bfloat16)).astype(jnp.float32)
        attended = jnp.einsum('abnh,abnhd->nhd', probs_low, value_window).astype(jnp.bfloat16)
        row_delta = jnp.sum(grad_row * attended.astype(jnp.float32), axis=2)
        grad_prob = jnp.einsum('nhd,abnhd->abnh', grad_row, value_window)
        grad_score = probs * (grad_prob - row_delta)
        grad_score = lax.optimization_barrier(grad_score.astype(jnp.bfloat16)).astype(jnp.float32)
        grad_query = jnp.einsum('abnh,abnhd->nhd', grad_score, key_window) * score_scale
        return (attended.reshape(NLON, INNER), grad_query.astype(jnp.bfloat16).reshape(NLON, INNER),
                log_norm, row_delta)

    row_ids = jnp.arange(NLAT, dtype=jnp.int32)
    attended, grad_queries, log_norm, row_delta = lax.map(forward_row, row_ids)

    queries_pad = pad_grid(queries)
    grad_pad = pad_grid(grad_attended)
    norm_pad = pad_grid(log_norm)
    delta_pad = pad_grid(row_delta)

    def key_row(lat_row):
        key_here = lax.dynamic_index_in_dim(keys, lat_row, 0, keepdims=False)
        key_here = key_here.astype(jnp.float32).reshape(NLON, HEADS, HEAD_DIM)
        value_here = lax.dynamic_index_in_dim(values, lat_row, 0, keepdims=False)
        value_here = value_here.astype(jnp.float32).reshape(NLON, HEADS, HEAD_DIM)
        query_window = split_heads(window_of(queries_pad, lat_row))
        grad_window = split_heads(window_of(grad_pad, lat_row))
        norm_window = window_of(norm_pad, lat_row)
        delta_window = window_of(delta_pad, lat_row)
        inside = rows_inside(lat_row)
        scores = jnp.einsum('nhd,abnhd->abnh', key_here, query_window) * score_scale
        probs = jnp.where(inside, jnp.exp(scores - norm_window), 0.0)
        probs_low = lax.optimization_barrier(probs.astype(jnp.bfloat16)).astype(jnp.float32)
        grad_value = jnp.einsum('abnh,abnhd->nhd', probs_low, grad_window).astype(jnp.bfloat16)
        grad_prob = jnp.einsum('nhd,abnhd->abnh', value_here, grad_window)
        grad_score = probs * (grad_prob - delta_window)
        grad_score = lax.optimization_barrier(grad_score.astype(jnp.bfloat16)).astype(jnp.float32)
        grad_key = jnp.einsum('abnh,abnhd->nhd', grad_score, query_window) * score_scale
        return grad_key.astype(jnp.bfloat16).reshape(NLON, INNER), grad_value.reshape(NLON, INNER)

    grad_keys, grad_values = lax.map(key_row, row_ids)
    attended_flat = attended.reshape(NLAT * NLON, INNER)
    grad_weight = jnp.dot(attended_flat.T, upstream_flat, preferred_element_type=jnp.float32) / NLAT
    return grad_queries, grad_keys, grad_values, grad_weight
```

```python
import functools

import jax
import jax.numpy as jnp
from jax import lax
from jax.experimental import pallas as pl
from jax.experimental.pallas import tpu as pltpu
from jax.sharding import PartitionSpec as P

HEADS = 8
RADIUS = 6
SIDE = 8
STRIP = 4
PACK = 4

NT = (((1,), (1,)), ((), ()))
NN = (((1,), (0,)), ((), ()))


def mm(a, b, dims):
    return lax.dot_general(a, b, dims, preferred_element_type=jnp.float32)


def attention_kernel(
    lat_total,
    base_ref,
    q_ref,
    g_ref,
    ext_ref,
    halo_ref,
    up_ref,
    dq_ref,
    own_ref,
    left_ref,
    right_ref,
    gw_ref,
    kv,
    kt,
    vt,
    acc,
    att_t,
    dq_t,
):
    rows, cols, inner = q_ref.shape
    ext_rows = rows + 2 * RADIUS
    wide = cols + 2 * SIDE
    head = inner // HEADS
    scale = head ** (-0.5)
    group = PACK * head
    strip_q = STRIP * cols
    slab_rows = STRIP + 2 * RADIUS
    slab = slab_rows * wide
    lanes = PACK * strip_q
    base = base_ref[0]

    kv[:, 0:cols, :] = ext_ref[...]
    kv[:, cols:wide, :] = halo_ref[...]
    kt[...] = kv[:, :, 0:inner].reshape(ext_rows * wide, inner).T
    vt[...] = kv[:, :, inner:].reshape(ext_rows * wide, inner).T
    acc[...] = jnp.zeros_like(acc)

    key = lax.broadcasted_iota(jnp.int32, (slab, lanes), 0)
    query = lax.broadcasted_iota(jnp.int32, (slab, lanes), 1) & (strip_q - 1)
    row = key // wide
    place = key & (wide - 1)
    col = jnp.where(
        place < cols, place, jnp.where(place < cols + SIDE, place - cols - SIDE, place - SIDE)
    )
    row_gap = row - query // cols
    col_gap = jnp.abs(col - (query & (cols - 1)))
    near = (row_gap >= 0) & (row_gap <= 2 * RADIUS) & (col_gap <= RADIUS)
    diag = (lax.broadcasted_iota(jnp.int32, (lanes, group), 0) // strip_q) == (
        lax.broadcasted_iota(jnp.int32, (lanes, group), 1) // head
    )

    def spread(block):
        tall = jnp.concatenate([block.astype(jnp.float32)] * PACK, axis=0)
        return jnp.where(diag, tall, 0.0).astype(jnp.bfloat16)

    def diagonal(square):
        return jnp.concatenate(
            [
                square[h * head : (h + 1) * head, h * strip_q : (h + 1) * strip_q]
                for h in range(PACK)
            ],
            axis=0,
        )

    for s in range(rows // STRIP):
        first = s * STRIP
        low = RADIUS - base - first
        allowed = near & (row >= low) & (row < low + lat_total)
        window = slice(first * wide, first * wide + slab)
        for part in range(HEADS // PACK):
            chans = slice(part * group, (part + 1) * group)
            vchans = slice(inner + part * group, inner + (part + 1) * group)
            keys = kv[first : first + slab_rows, :, chans].reshape(slab, group)
            values = kv[first : first + slab_rows, :, vchans].reshape(slab, group)
            q_wide = spread(
                q_ref[first : first + STRIP, :, chans].reshape(strip_q, group) * scale
            )
            g_wide = spread(g_ref[first : first + STRIP, :, chans].reshape(strip_q, group))
            scores = jnp.where(allowed, mm(keys, q_wide, NT), -1e30)
            weights = jnp.exp(scores - jnp.max(scores, axis=0, keepdims=True))
            probs = weights * (1.0 / jnp.sum(weights, axis=0, keepdims=True))
            low_probs = probs.astype(jnp.bfloat16)
            grad_prob = mm(values, g_wide, NT)
            delta = jnp.sum(low_probs.astype(jnp.float32) * grad_prob, axis=0, keepdims=True)
            grad_score = (probs * (grad_prob - delta)).astype(jnp.bfloat16)
            here = slice(s * strip_q, (s + 1) * strip_q)
            att_t[chans, here] = diagonal(mm(vt[chans, window], low_probs, NN))
            dq_t[chans, here] = diagonal(mm(kt[chans, window], grad_score, NN)) * scale
            acc[first : first + slab_rows, :, chans] += mm(grad_score, q_wide, NN).reshape(
                slab_rows, wide, group
            )
            acc[first : first + slab_rows, :, vchans] += mm(low_probs, g_wide, NN).reshape(
                slab_rows, wide, group
            )

    dq_ref[...] = dq_t[...].T.astype(jnp.bfloat16).reshape(rows, cols, inner)
    own_ref[...] = acc[:, 0:cols, :]
    left_ref[...] = acc[:, cols : cols + SIDE, :].astype(jnp.bfloat16)
    right_ref[...] = acc[:, cols + SIDE : wide, :].astype(jnp.bfloat16)
    gw_ref[...] = mm(att_t[...].astype(jnp.bfloat16), up_ref[...], NN).astype(jnp.bfloat16)


def attention(base, queries, grads, extended, halo, upstream, lat_total, interpret=False):
    rows, cols, inner = queries.shape
    ext_rows = rows + 2 * RADIUS
    wide = cols + 2 * SIDE
    tokens = rows * cols
    model = upstream.shape[1]
    vmem = pl.BlockSpec(memory_space=pltpu.VMEM)
    return pl.pallas_call(
        functools.partial(attention_kernel, lat_total),
        out_shape=(
            jax.ShapeDtypeStruct((rows, cols, inner), jnp.bfloat16),
            jax.ShapeDtypeStruct((ext_rows, cols, 2 * inner), jnp.float32),
            jax.ShapeDtypeStruct((ext_rows, SIDE, 2 * inner), jnp.bfloat16),
            jax.ShapeDtypeStruct((ext_rows, SIDE, 2 * inner), jnp.bfloat16),
            jax.ShapeDtypeStruct((inner, model), jnp.bfloat16),
        ),
        in_specs=[pl.BlockSpec(memory_space=pltpu.SMEM)] + [vmem] * 5,
        out_specs=(vmem,) * 5,
        scratch_shapes=[
            pltpu.VMEM((ext_rows, wide, 2 * inner), jnp.bfloat16),
            pltpu.VMEM((inner, ext_rows * wide), jnp.bfloat16),
            pltpu.VMEM((inner, ext_rows * wide), jnp.bfloat16),
            pltpu.VMEM((ext_rows, wide, 2 * inner), jnp.float32),
            pltpu.VMEM((inner, tokens), jnp.float32),
            pltpu.VMEM((inner, tokens), jnp.float32),
        ],
        compiler_params=pltpu.CompilerParams(vmem_limit_bytes=48 << 20),
        cost_estimate=pl.CostEstimate(
            flops=2_600_000_000, bytes_accessed=8_000_000, transcendentals=800_000
        ),
        interpret=interpret,
    )(base, queries, grads, extended, halo, upstream)


def ring(block, axis, by):
    size = lax.axis_size(axis)
    return lax.ppermute(block, axis, [(i, (i + by) % size) for i in range(size)])


def line(block, axis, by):
    size = lax.axis_size(axis)
    return lax.ppermute(
        block, axis, [(i, i + by) for i in range(size) if 0 <= i + by < size]
    )


def reduce_weight(part, out_rows):
    lon = lax.axis_size("lon")
    me = lax.axis_index("lon")
    model = part.shape[1]
    cores, near = 2, 4
    far = lon // (cores * near)
    core = me % cores
    blocks = part.reshape(far, near, cores, out_rows, model)
    keep = lax.dynamic_index_in_dim(blocks, core, 2, keepdims=False)
    give = lax.dynamic_index_in_dim(blocks, 1 - core, 2, keepdims=False)
    got = lax.ppermute(give, "lon", [(i, i ^ 1) for i in range(lon)])
    half = (keep.astype(jnp.float32) + got.astype(jnp.float32)).astype(jnp.bfloat16)
    stride = near * cores
    far_groups = [[j + stride * i for i in range(far)] for j in range(stride)]
    split = lax.all_to_all(
        half.reshape(far, near * out_rows, model), "lon", 0, 0, axis_index_groups=far_groups, tiled=True
    )
    quarter = jnp.sum(split.astype(jnp.float32), axis=0).astype(jnp.bfloat16)
    near_groups = [
        [f * stride + n * cores + c for n in range(near)] for f in range(far) for c in range(cores)
    ]
    split = lax.all_to_all(
        quarter.reshape(near, out_rows, model), "lon", 0, 0, axis_index_groups=near_groups, tiled=True
    )
    share = jnp.sum(split.astype(jnp.float32), axis=0).astype(jnp.bfloat16)
    lat = lax.axis_size("lat")
    copies = jnp.broadcast_to(share[None], (lat,) + share.shape)
    every = lax.all_to_all(copies, "lat", 0, 0, tiled=True)
    return jnp.sum(every.astype(jnp.float32), axis=0)


def shards(queries, keys, values, upstream, out_weight):
    rows, cols, inner = queries.shape
    model = upstream.shape[2]
    tokens = rows * cols
    lat_total = rows * lax.axis_size("lat")
    base = (lax.axis_index("lat") * rows).astype(jnp.int32).reshape(1)
    up_flat = upstream.reshape(tokens, model)
    grads = (
        jnp.einsum("td,id->ti", up_flat, out_weight, preferred_element_type=jnp.float32)
        .astype(jnp.bfloat16)
        .reshape(rows, cols, inner)
    )
    both = jnp.concatenate([keys, values], axis=2)
    above = ring(both[rows - RADIUS :], "lat", 1)
    below = ring(both[:RADIUS], "lat", -1)
    extended = jnp.concatenate([above, both, below], axis=0)
    west = ring(extended[:, cols - SIDE :], "lon", 1)
    east = ring(extended[:, :SIDE], "lon", -1)
    halo = jnp.concatenate([west, east], axis=1)
    grad_query, own, left, right, weight_term = attention(
        base, queries, grads, extended, halo, up_flat, lat_total
    )
    from_east = ring(left, "lon", -1)
    from_west = ring(right, "lon", 1)
    sums = own + jnp.concatenate([from_west, from_east], axis=1).astype(jnp.float32)
    from_below = line(sums[:RADIUS].astype(jnp.bfloat16), "lat", -1)
    from_above = line(sums[RADIUS + rows :].astype(jnp.bfloat16), "lat", 1)
    owned = sums[RADIUS : RADIUS + rows] + jnp.concatenate(
        [from_above, from_below], axis=0
    ).astype(jnp.float32)
    grad_key = owned[:, :, :inner].astype(jnp.bfloat16)
    grad_value = owned[:, :, inner:].astype(jnp.bfloat16)
    grad_weight = reduce_weight(weight_term, inner // lax.axis_size("lon")) / lat_total
    return (grad_query, grad_key, grad_value, grad_weight)


def solution(mesh):
    placed = P("lat", "lon", None)
    return jax.shard_map(
        shards,
        mesh=mesh,
        in_specs=(placed, placed, placed, placed, P()),
        out_specs=(placed, placed, placed, P("lon", None)),
        check_vma=False,
    )
```

```python
import functools

import jax
import jax.numpy as jnp
from jax import lax
from jax.experimental import pallas as pl
from jax.experimental.pallas import tpu as pltpu
from jax.sharding import PartitionSpec as P

HEADS = 8
RADIUS = 6
SIDE = 8
STRIP = 4
PACK = 4

NT = (((1,), (1,)), ((), ()))
NN = (((1,), (0,)), ((), ()))


def mm(a, b, dims):
    return lax.dot_general(a, b, dims, preferred_element_type=jnp.float32)


def spread(block, diag):
    tall = jnp.concatenate([block.astype(jnp.float32)] * PACK, axis=0)
    return jnp.where(diag, tall, 0.0).astype(jnp.bfloat16)


def diagonal(square, head, strip_q):
    return jnp.concatenate(
        [square[h * head : (h + 1) * head, h * strip_q : (h + 1) * strip_q] for h in range(PACK)],
        axis=0,
    )


def masks(rows, cols, inner):
    head = inner // HEADS
    wide = cols + 2 * SIDE
    strip_q = STRIP * cols
    slab = (STRIP + 2 * RADIUS) * wide
    lanes = PACK * strip_q
    key = lax.broadcasted_iota(jnp.int32, (slab, lanes), 0)
    query = lax.broadcasted_iota(jnp.int32, (slab, lanes), 1) & (strip_q - 1)
    row = key // wide
    place = key & (wide - 1)
    col = jnp.where(
        place < cols, place, jnp.where(place < cols + SIDE, place - cols - SIDE, place - SIDE)
    )
    row_gap = row - query // cols
    col_gap = jnp.abs(col - (query & (cols - 1)))
    near = (row_gap >= 0) & (row_gap <= 2 * RADIUS) & (col_gap <= RADIUS)
    diag = (lax.broadcasted_iota(jnp.int32, (lanes, PACK * head), 0) // strip_q) == (
        lax.broadcasted_iota(jnp.int32, (lanes, PACK * head), 1) // head
    )
    return near, row, diag


def forward_kernel(
    lat_total, place_ref, q_ref, ext_ref, west_ref, east_ref, up_ref,
    kv_ref, norm_ref, keep_ref, give_ref, vt, att_t,
):
    rows, cols, inner = q_ref.shape
    ext_rows = rows + 2 * RADIUS
    wide = cols + 2 * SIDE
    head = inner // HEADS
    scale = head ** (-0.5)
    group = PACK * head
    strip_q = STRIP * cols
    slab_rows = STRIP + 2 * RADIUS
    slab = slab_rows * wide
    base, core = place_ref[0], place_ref[1]

    kv_ref[:, 0:cols, :] = ext_ref[...]
    kv_ref[:, cols:wide, :] = jnp.concatenate(
        [west_ref[...].astype(jnp.float32), east_ref[...].astype(jnp.float32)], axis=1
    ).astype(jnp.bfloat16)
    vt[...] = kv_ref[:, :, inner:].reshape(ext_rows * wide, inner).T
    near, row, diag = masks(rows, cols, inner)

    for s in range(rows // STRIP):
        first = s * STRIP
        low = RADIUS - base - first
        allowed = near & (row >= low) & (row < low + lat_total)
        window = slice(first * wide, first * wide + slab)
        here = slice(s * strip_q, (s + 1) * strip_q)
        for part in range(HEADS // PACK):
            chans = slice(part * group, (part + 1) * group)
            keys = kv_ref[first : first + slab_rows, :, chans].reshape(slab, group)
            q_wide = spread(
                q_ref[first : first + STRIP, :, chans].reshape(strip_q, group) * scale, diag
            )
            scores = jnp.where(allowed, mm(keys, q_wide, NT), -1e30)
            top = jnp.max(scores, axis=0, keepdims=True)
            weights = jnp.exp(scores - top)
            total = jnp.sum(weights, axis=0, keepdims=True)
            probs = (weights * (1.0 / total)).astype(jnp.bfloat16)
            at = s * (HEADS // PACK) + part
            norm_ref[at : at + 1, :] = top + jnp.log(total)
            att_t[chans, here] = diagonal(mm(vt[chans, window], probs, NN), head, strip_q)

    weight = mm(att_t[...].astype(jnp.bfloat16), up_ref[...], NN)
    out_rows = keep_ref.shape[1]
    weight = weight.reshape(keep_ref.shape[0], 2, out_rows, weight.shape[1])
    keep_ref[...] = jnp.where(core == 0, weight[:, 0], weight[:, 1])
    give_ref[...] = jnp.where(core == 0, weight[:, 1], weight[:, 0]).astype(jnp.bfloat16)


def backward_kernel(
    lat_total, place_ref, q_ref, g_ref, kv_ref, norm_ref,
    dq_ref, mid_k_ref, mid_v_ref, rim_ref, left_ref, right_ref, kt, acc, dq_t,
):
    rows, cols, inner = q_ref.shape
    ext_rows = rows + 2 * RADIUS
    wide = cols + 2 * SIDE
    head = inner // HEADS
    scale = head ** (-0.5)
    group = PACK * head
    strip_q = STRIP * cols
    slab_rows = STRIP + 2 * RADIUS
    slab = slab_rows * wide
    base = place_ref[0]

    kt[...] = kv_ref[:, :, 0:inner].reshape(ext_rows * wide, inner).T
    acc[...] = jnp.zeros_like(acc)
    near, row, diag = masks(rows, cols, inner)

    for s in range(rows // STRIP):
        first = s * STRIP
        low = RADIUS - base - first
        allowed = near & (row >= low) & (row < low + lat_total)
        window = slice(first * wide, first * wide + slab)
        here = slice(s * strip_q, (s + 1) * strip_q)
        for part in range(HEADS // PACK):
            chans = slice(part * group, (part + 1) * group)
            vchans = slice(inner + part * group, inner + (part + 1) * group)
            keys = kv_ref[first : first + slab_rows, :, chans].reshape(slab, group)
            values = kv_ref[first : first + slab_rows, :, vchans].reshape(slab, group)
            q_wide = spread(
                q_ref[first : first + STRIP, :, chans].reshape(strip_q, group) * scale, diag
            )
            g_wide = spread(g_ref[first : first + STRIP, :, chans].reshape(strip_q, group), diag)
            at = s * (HEADS // PACK) + part
            scores = jnp.where(allowed, mm(keys, q_wide, NT), -1e30)
            probs = jnp.exp(scores - norm_ref[at : at + 1, :])
            low_probs = probs.astype(jnp.bfloat16)
            grad_prob = mm(values, g_wide, NT)
            delta = jnp.sum(low_probs.astype(jnp.float32) * grad_prob, axis=0, keepdims=True)
            grad_score = (probs * (grad_prob - delta)).astype(jnp.bfloat16)
            dq_t[chans, here] = diagonal(mm(kt[chans, window], grad_score, NN), head, strip_q) * scale
            acc[first : first + slab_rows, :, chans] += mm(grad_score, q_wide, NN).reshape(
                slab_rows, wide, group
            )
            acc[first : first + slab_rows, :, vchans] += mm(low_probs, g_wide, NN).reshape(
                slab_rows, wide, group
            )

    left_ref[...] = acc[:, cols : cols + SIDE, :].astype(jnp.bfloat16)
    right_ref[...] = acc[:, cols + SIDE : wide, :].astype(jnp.bfloat16)
    rim_ref[0:RADIUS] = acc[0:RADIUS, 0:cols, :]
    rim_ref[RADIUS:] = acc[RADIUS + rows :, 0:cols, :]
    mid_k_ref[...] = acc[RADIUS : RADIUS + rows, 0:cols, 0:inner]
    mid_v_ref[...] = acc[RADIUS : RADIUS + rows, 0:cols, inner:]
    dq_ref[...] = dq_t[...].T.astype(jnp.bfloat16).reshape(rows, cols, inner)


def share_kernel(parts_ref, copies_ref):
    total = jnp.sum(parts_ref[...].astype(jnp.float32), axis=0).astype(jnp.bfloat16)
    copies_ref[...] = jnp.broadcast_to(total[None], copies_ref.shape)


def pack_kernel(keys_ref, values_ref, both_ref):
    inner = keys_ref.shape[2]
    both_ref[:, :, 0:inner] = keys_ref[...]
    both_ref[:, :, inner:] = values_ref[...]


def wide(block):
    return block.astype(jnp.float32)


def rim_kernel(rim_ref, west_ref, east_ref, top_ref, bottom_ref):
    deep = top_ref.shape[0]
    for out, at, there in (
        (top_ref, 0, 0),
        (bottom_ref, deep, west_ref.shape[0] - deep),
    ):
        side = jnp.concatenate(
            [wide(west_ref[there : there + deep]), wide(east_ref[there : there + deep])], axis=1
        )
        out[...] = (rim_ref[at : at + deep] + side).astype(jnp.bfloat16)


def finish_kernel(
    mid_k_ref, mid_v_ref, west_ref, east_ref, above_ref, below_ref, keys_ref, values_ref
):
    inner = mid_k_ref.shape[2]
    deep = above_ref.shape[0]
    for out, mid, chans in (
        (keys_ref, mid_k_ref, slice(0, inner)),
        (values_ref, mid_v_ref, slice(inner, 2 * inner)),
    ):
        for at, pole in ((0, above_ref), (deep, below_ref)):
            there = slice(deep + at, 2 * deep + at)
            side = jnp.concatenate(
                [wide(west_ref[there, :, chans]), wide(east_ref[there, :, chans])], axis=1
            )
            total = mid[at : at + deep] + side + wide(pole[:, :, chans])
            out[at : at + deep] = total.astype(jnp.bfloat16)


VMEM = pl.BlockSpec(memory_space=pltpu.VMEM)
SMEM = pl.BlockSpec(memory_space=pltpu.SMEM)
PARAMS = pltpu.CompilerParams(vmem_limit_bytes=20 << 20)
SMALL = pltpu.CompilerParams(vmem_limit_bytes=8 << 20)


def shape(dims, kind=jnp.bfloat16):
    return jax.ShapeDtypeStruct(dims, kind)


def forward(place, queries, extended, west, east, upstream, lat_total, out_rows):
    rows, cols, inner = queries.shape
    ext_rows, wide = rows + 2 * RADIUS, cols + 2 * SIDE
    model = upstream.shape[1]
    return pl.pallas_call(
        functools.partial(forward_kernel, lat_total),
        out_shape=(
            shape((ext_rows, wide, 2 * inner)),
            shape((8, PACK * STRIP * cols), jnp.float32),
            shape((inner // (2 * out_rows), out_rows, model), jnp.float32),
            shape((inner // (2 * out_rows), out_rows, model)),
        ),
        in_specs=[SMEM] + [VMEM] * 5,
        out_specs=(VMEM,) * 4,
        scratch_shapes=[
            pltpu.VMEM((inner, ext_rows * wide), jnp.bfloat16),
            pltpu.VMEM((inner, rows * cols), jnp.float32),
        ],
        compiler_params=PARAMS,
        cost_estimate=pl.CostEstimate(
            flops=1_000_000_000, bytes_accessed=5_000_000, transcendentals=800_000
        ),
        name="forward",
    )(place, queries, extended, west, east, upstream)


def backward(place, queries, grads, kv, norm, lat_total):
    rows, cols, inner = queries.shape
    ext_rows, wide = rows + 2 * RADIUS, cols + 2 * SIDE
    return pl.pallas_call(
        functools.partial(backward_kernel, lat_total),
        out_shape=(
            shape((rows, cols, inner)),
            shape((rows, cols, inner), jnp.float32),
            shape((rows, cols, inner), jnp.float32),
            shape((2 * RADIUS, cols, 2 * inner), jnp.float32),
            shape((ext_rows, SIDE, 2 * inner)),
            shape((ext_rows, SIDE, 2 * inner)),
        ),
        in_specs=[SMEM] + [VMEM] * 4,
        out_specs=(VMEM,) * 6,
        scratch_shapes=[
            pltpu.VMEM((inner, ext_rows * wide), jnp.bfloat16),
            pltpu.VMEM((ext_rows, wide, 2 * inner), jnp.float32),
            pltpu.VMEM((inner, rows * cols), jnp.float32),
        ],
        compiler_params=PARAMS,
        cost_estimate=pl.CostEstimate(
            flops=20_000_000_000, bytes_accessed=70_000_000, transcendentals=800_000
        ),
        name="backward",
    )(place, queries, grads, kv, norm)


def ring(block, axis, by):
    size = lax.axis_size(axis)
    return lax.ppermute(block, axis, [(i, (i + by) % size) for i in range(size)])


def line(block, axis, by):
    size = lax.axis_size(axis)
    return lax.ppermute(
        block, axis, [(i, i + by) for i in range(size) if 0 <= i + by < size]
    )


def shards(queries, keys, values, upstream, out_weight):
    rows, cols, inner = queries.shape
    model = upstream.shape[2]
    tokens = rows * cols
    lat, lon = lax.axis_size("lat"), lax.axis_size("lon")
    lat_total = rows * lat
    out_rows = inner // lon
    place = jnp.stack([lax.axis_index("lat") * rows, lax.axis_index("lon") % 2]).astype(jnp.int32)
    up_flat = upstream.reshape(tokens, model)
    grads = (
        jnp.einsum("td,id->ti", up_flat, out_weight, preferred_element_type=jnp.float32)
        .astype(jnp.bfloat16)
        .reshape(rows, cols, inner)
    )
    both = pl.pallas_call(
        pack_kernel, out_shape=shape((rows, cols, 2 * inner)), name="pack", compiler_params=SMALL
    )(keys, values)
    above = line(both[rows - RADIUS :], "lat", 1)
    below = line(both[:RADIUS], "lat", -1)
    extended = jnp.concatenate([above, both, below], axis=0)
    west = ring(extended[:, cols - SIDE :], "lon", 1)
    east = ring(extended[:, :SIDE], "lon", -1)
    kv, norm, keep, give = forward(
        place, queries, extended, west, east, up_flat, lat_total, out_rows
    )
    got = lax.ppermute(give, "lon", [(i, i ^ 1) for i in range(lon)])
    half = (keep + got.astype(jnp.float32)).astype(jnp.bfloat16)
    same_core = [[2 * i + c for i in range(lon // 2)] for c in range(2)]
    terms = lax.all_to_all(half, "lon", 0, 0, axis_index_groups=same_core, tiled=True)

    grad_query, mid_k, mid_v, rim, left, right = backward(
        place, queries, grads, kv, norm, lat_total
    )
    from_east = ring(left, "lon", -1)
    from_west = ring(right, "lon", 1)
    rim, _ = lax.optimization_barrier((rim, half))
    top, bottom = pl.pallas_call(
        rim_kernel,
        out_shape=(shape((RADIUS, cols, 2 * inner)),) * 2,
        name="rim", compiler_params=SMALL,
    )(rim, from_west, from_east)
    from_below = line(top, "lat", -1)
    from_above = line(bottom, "lat", 1)
    terms, _ = lax.optimization_barrier((terms, top))
    copies = pl.pallas_call(
        share_kernel, out_shape=shape((lat, out_rows, model)), name="share", compiler_params=SMALL
    )(terms)
    every = lax.all_to_all(copies, "lat", 0, 0, tiled=True)
    grad_weight = jnp.sum(every.astype(jnp.float32), axis=0) / lat_total
    mid_k, mid_v, _ = lax.optimization_barrier((mid_k, mid_v, copies))
    grad_key, grad_value = pl.pallas_call(
        finish_kernel,
        out_shape=(shape((rows, cols, inner)),) * 2,
        name="finish", compiler_params=SMALL,
        cost_estimate=pl.CostEstimate(flops=50_000_000_000, bytes_accessed=4_000_000, transcendentals=0),
    )(mid_k, mid_v, from_west, from_east, from_above, from_below)
    return (grad_query, grad_key, grad_value, grad_weight)


def solution(mesh):
    placed = P("lat", "lon", None)
    return jax.shard_map(
        shards,
        mesh=mesh,
        in_specs=(placed, placed, placed, placed, P()),
        out_specs=(placed, placed, placed, P("lon", None)),
        check_vma=False,
    )
```

```python
import functools

import jax
import jax.numpy as jnp
from jax import lax
from jax.experimental import pallas as pl
from jax.experimental.pallas import tpu as pltpu
from jax.sharding import PartitionSpec as P

HEADS = 8
RADIUS = 6
SIDE = 8
STRIP = 4
PACK = 4

NT = (((1,), (1,)), ((), ()))
NN = (((1,), (0,)), ((), ()))


def mm(a, b, dims):
    return lax.dot_general(a, b, dims, preferred_element_type=jnp.float32)


def spread(block, diag):
    tall = jnp.concatenate([block.astype(jnp.float32)] * PACK, axis=0)
    return jnp.where(diag, tall, 0.0).astype(jnp.bfloat16)


def diagonal(square, head, strip_q):
    return jnp.concatenate(
        [square[h * head : (h + 1) * head, h * strip_q : (h + 1) * strip_q] for h in range(PACK)],
        axis=0,
    )


def masks(rows, cols, inner):
    head = inner // HEADS
    wide = cols + 2 * SIDE
    strip_q = STRIP * cols
    slab = (STRIP + 2 * RADIUS) * wide
    lanes = PACK * strip_q
    key = lax.broadcasted_iota(jnp.int32, (slab, lanes), 0)
    query = lax.broadcasted_iota(jnp.int32, (slab, lanes), 1) & (strip_q - 1)
    row = key // wide
    place = key & (wide - 1)
    col = jnp.where(
        place < cols, place, jnp.where(place < cols + SIDE, place - cols - SIDE, place - SIDE)
    )
    row_gap = row - query // cols
    col_gap = jnp.abs(col - (query & (cols - 1)))
    near = (row_gap >= 0) & (row_gap <= 2 * RADIUS) & (col_gap <= RADIUS)
    diag = (lax.broadcasted_iota(jnp.int32, (lanes, PACK * head), 0) // strip_q) == (
        lax.broadcasted_iota(jnp.int32, (lanes, PACK * head), 1) // head
    )
    return near, row, diag


def forward_kernel(
    lat_total, place_ref, q_ref, ext_ref, west_ref, east_ref, up_ref,
    kv_ref, norm_ref, keep_ref, give_ref, vt, att_t,
):
    rows, cols, inner = q_ref.shape
    ext_rows = rows + 2 * RADIUS
    wide = cols + 2 * SIDE
    head = inner // HEADS
    scale = head ** (-0.5)
    group = PACK * head
    strip_q = STRIP * cols
    slab_rows = STRIP + 2 * RADIUS
    slab = slab_rows * wide
    base, core = place_ref[0], place_ref[1]

    kv_ref[:, 0:cols, :] = ext_ref[...]
    kv_ref[:, cols:wide, :] = jnp.concatenate(
        [west_ref[...].astype(jnp.float32), east_ref[...].astype(jnp.float32)], axis=1
    ).astype(jnp.bfloat16)
    vt[...] = kv_ref[:, :, inner:].reshape(ext_rows * wide, inner).T
    near, row, diag = masks(rows, cols, inner)

    for s in range(rows // STRIP):
        first = s * STRIP
        low = RADIUS - base - first
        allowed = near & (row >= low) & (row < low + lat_total)
        window = slice(first * wide, first * wide + slab)
        here = slice(s * strip_q, (s + 1) * strip_q)
        for part in range(HEADS // PACK):
            chans = slice(part * group, (part + 1) * group)
            keys = kv_ref[first : first + slab_rows, :, chans].reshape(slab, group)
            q_wide = spread(
                q_ref[first : first + STRIP, :, chans].reshape(strip_q, group) * scale, diag
            )
            scores = jnp.where(allowed, mm(keys, q_wide, NT), -1e30)
            top = jnp.max(scores, axis=0, keepdims=True)
            weights = jnp.exp(scores - top)
            total = jnp.sum(weights, axis=0, keepdims=True)
            probs = (weights * (1.0 / total)).astype(jnp.bfloat16)
            at = s * (HEADS // PACK) + part
            norm_ref[at : at + 1, :] = top + jnp.log(total)
            att_t[chans, here] = diagonal(mm(vt[chans, window], probs, NN), head, strip_q)

    weight = mm(att_t[...].astype(jnp.bfloat16), up_ref[...], NN)
    out_rows = keep_ref.shape[1]
    weight = weight.reshape(keep_ref.shape[0], 2, out_rows, weight.shape[1])
    keep_ref[...] = jnp.where(core == 0, weight[:, 0], weight[:, 1])
    give_ref[...] = jnp.where(core == 0, weight[:, 1], weight[:, 0]).astype(jnp.bfloat16)


def backward_kernel(
    lat_total, place_ref, q_ref, g_ref, kv_ref, norm_ref,
    dq_ref, mid_ref, rim_ref, left_ref, right_ref, kt, acc, dq_t,
):
    rows, cols, inner = q_ref.shape
    ext_rows = rows + 2 * RADIUS
    wide = cols + 2 * SIDE
    head = inner // HEADS
    scale = head ** (-0.5)
    group = PACK * head
    strip_q = STRIP * cols
    slab_rows = STRIP + 2 * RADIUS
    slab = slab_rows * wide
    base = place_ref[0]

    kt[...] = kv_ref[:, :, 0:inner].reshape(ext_rows * wide, inner).T
    acc[...] = jnp.zeros_like(acc)
    near, row, diag = masks(rows, cols, inner)

    for s in range(rows // STRIP):
        first = s * STRIP
        low = RADIUS - base - first
        allowed = near & (row >= low) & (row < low + lat_total)
        window = slice(first * wide, first * wide + slab)
        here = slice(s * strip_q, (s + 1) * strip_q)
        for part in range(HEADS // PACK):
            chans = slice(part * group, (part + 1) * group)
            vchans = slice(inner + part * group, inner + (part + 1) * group)
            keys = kv_ref[first : first + slab_rows, :, chans].reshape(slab, group)
            values = kv_ref[first : first + slab_rows, :, vchans].reshape(slab, group)
            q_wide = spread(
                q_ref[first : first + STRIP, :, chans].reshape(strip_q, group) * scale, diag
            )
            g_wide = spread(g_ref[first : first + STRIP, :, chans].reshape(strip_q, group), diag)
            at = s * (HEADS // PACK) + part
            scores = jnp.where(allowed, mm(keys, q_wide, NT), -1e30)
            probs = jnp.exp(scores - norm_ref[at : at + 1, :])
            low_probs = probs.astype(jnp.bfloat16)
            grad_prob = mm(values, g_wide, NT)
            delta = jnp.sum(low_probs.astype(jnp.float32) * grad_prob, axis=0, keepdims=True)
            grad_score = (probs * (grad_prob - delta)).astype(jnp.bfloat16)
            dq_t[chans, here] = diagonal(mm(kt[chans, window], grad_score, NN), head, strip_q) * scale
            acc[first : first + slab_rows, :, chans] += mm(grad_score, q_wide, NN).reshape(
                slab_rows, wide, group
            )
            acc[first : first + slab_rows, :, vchans] += mm(low_probs, g_wide, NN).reshape(
                slab_rows, wide, group
            )

    left_ref[...] = acc[:, cols : cols + SIDE, :].astype(jnp.bfloat16)
    right_ref[...] = acc[:, cols + SIDE : wide, :].astype(jnp.bfloat16)
    rim_ref[0:RADIUS] = acc[0:RADIUS, 0:cols, :].astype(jnp.bfloat16)
    rim_ref[RADIUS:] = acc[RADIUS + rows :, 0:cols, :].astype(jnp.bfloat16)
    mid_ref[...] = acc[RADIUS : RADIUS + rows, 0:cols, :].astype(jnp.bfloat16)
    dq_ref[...] = dq_t[...].T.astype(jnp.bfloat16).reshape(rows, cols, inner)


def share_kernel(parts_ref, copies_ref):
    total = jnp.sum(parts_ref[...].astype(jnp.float32), axis=0).astype(jnp.bfloat16)
    copies_ref[...] = jnp.broadcast_to(total[None], copies_ref.shape)


def pack_kernel(keys_ref, values_ref, both_ref, sems):
    inner = keys_ref.shape[2]
    copies = [
        pltpu.make_async_copy(keys_ref, both_ref.at[:, :, pl.ds(0, inner)], sems.at[0]),
        pltpu.make_async_copy(values_ref, both_ref.at[:, :, pl.ds(inner, inner)], sems.at[1]),
    ]
    for copy in copies:
        copy.start()
    for copy in copies:
        copy.wait()


def fold_kernel(keep_ref, got_ref, half_ref):
    half_ref[...] = (keep_ref[...] + got_ref[...].astype(jnp.float32)).astype(jnp.bfloat16)


def mean_kernel(parts, terms_ref, out_ref):
    out_ref[...] = jnp.sum(terms_ref[...].astype(jnp.float32), axis=0) / parts


def wide(block):
    return block.astype(jnp.float32)


def rim_kernel(rim_ref, west_ref, east_ref, top_ref, bottom_ref):
    deep = top_ref.shape[0]
    for out, at, there in (
        (top_ref, 0, 0),
        (bottom_ref, deep, west_ref.shape[0] - deep),
    ):
        side = jnp.concatenate(
            [wide(west_ref[there : there + deep]), wide(east_ref[there : there + deep])], axis=1
        )
        out[...] = (wide(rim_ref[at : at + deep]) + side).astype(jnp.bfloat16)


def finish_kernel(
    mid_ref, west_ref, east_ref, above_ref, below_ref, keys_ref, values_ref
):
    inner = keys_ref.shape[2]
    deep = above_ref.shape[0]
    for out, chans in ((keys_ref, slice(0, inner)), (values_ref, slice(inner, 2 * inner))):
        for at, pole in ((0, above_ref), (deep, below_ref)):
            there = slice(deep + at, 2 * deep + at)
            side = jnp.concatenate(
                [wide(west_ref[there, :, chans]), wide(east_ref[there, :, chans])], axis=1
            )
            total = wide(mid_ref[at : at + deep, :, chans]) + side + wide(pole[:, :, chans])
            out[at : at + deep] = total.astype(jnp.bfloat16)


VMEM = pl.BlockSpec(memory_space=pltpu.VMEM)
SMEM = pl.BlockSpec(memory_space=pltpu.SMEM)
PARAMS = pltpu.CompilerParams(vmem_limit_bytes=20 << 20)
FOLD, RIM, FINISH = 6_000_000_000, 6_000_000_000, 6_000_000_000
SMALL = pltpu.CompilerParams(vmem_limit_bytes=8 << 20)


def shape(dims, kind=jnp.bfloat16):
    return jax.ShapeDtypeStruct(dims, kind)


def forward(place, queries, extended, west, east, upstream, lat_total, out_rows):
    rows, cols, inner = queries.shape
    ext_rows, wide = rows + 2 * RADIUS, cols + 2 * SIDE
    model = upstream.shape[1]
    return pl.pallas_call(
        functools.partial(forward_kernel, lat_total),
        out_shape=(
            shape((ext_rows, wide, 2 * inner)),
            shape((8, PACK * STRIP * cols), jnp.float32),
            shape((inner // (2 * out_rows), out_rows, model), jnp.float32),
            shape((inner // (2 * out_rows), out_rows, model)),
        ),
        in_specs=[SMEM] + [VMEM] * 5,
        out_specs=(VMEM,) * 4,
        scratch_shapes=[
            pltpu.VMEM((inner, ext_rows * wide), jnp.bfloat16),
            pltpu.VMEM((inner, rows * cols), jnp.float32),
        ],
        compiler_params=PARAMS,
        cost_estimate=pl.CostEstimate(
            flops=1_000_000_000, bytes_accessed=5_000_000, transcendentals=800_000
        ),
        name="forward",
    )(place, queries, extended, west, east, upstream)


def backward(place, queries, grads, kv, norm, lat_total):
    rows, cols, inner = queries.shape
    ext_rows, wide = rows + 2 * RADIUS, cols + 2 * SIDE
    return pl.pallas_call(
        functools.partial(backward_kernel, lat_total),
        out_shape=(
            shape((rows, cols, inner)),
            shape((rows, cols, 2 * inner)),
            shape((2 * RADIUS, cols, 2 * inner)),
            shape((ext_rows, SIDE, 2 * inner)),
            shape((ext_rows, SIDE, 2 * inner)),
        ),
        in_specs=[SMEM] + [VMEM] * 4,
        out_specs=(VMEM,) * 5,
        scratch_shapes=[
            pltpu.VMEM((inner, ext_rows * wide), jnp.bfloat16),
            pltpu.VMEM((ext_rows, wide, 2 * inner), jnp.float32),
            pltpu.VMEM((inner, rows * cols), jnp.float32),
        ],
        compiler_params=PARAMS,
        cost_estimate=pl.CostEstimate(
            flops=20_000_000_000, bytes_accessed=70_000_000, transcendentals=800_000
        ),
        name="backward",
    )(place, queries, grads, kv, norm)


def ring(block, axis, by):
    size = lax.axis_size(axis)
    return lax.ppermute(block, axis, [(i, (i + by) % size) for i in range(size)])


def line(block, axis, by):
    size = lax.axis_size(axis)
    return lax.ppermute(
        block, axis, [(i, i + by) for i in range(size) if 0 <= i + by < size]
    )


def cost(flops):
    return pl.CostEstimate(flops=flops, bytes_accessed=4_000_000, transcendentals=0)


def shards(queries, keys, values, upstream, out_weight):
    rows, cols, inner = queries.shape
    model = upstream.shape[2]
    tokens = rows * cols
    lat, lon = lax.axis_size("lat"), lax.axis_size("lon")
    lat_total = rows * lat
    out_rows = inner // lon
    place = jnp.stack([lax.axis_index("lat") * rows, lax.axis_index("lon") % 2]).astype(jnp.int32)
    up_flat = upstream.reshape(tokens, model)
    grads = (
        jnp.einsum("td,id->ti", up_flat, out_weight, preferred_element_type=jnp.float32)
        .astype(jnp.bfloat16)
        .reshape(rows, cols, inner)
    )
    both = pl.pallas_call(
        pack_kernel,
        out_shape=shape((rows, cols, 2 * inner)),
        in_specs=[pl.BlockSpec(memory_space=pl.ANY)] * 2,
        out_specs=VMEM,
        scratch_shapes=[pltpu.SemaphoreType.DMA((2,))],
        compiler_params=SMALL,
        name="pack",
    )(keys, values)
    above = line(both[rows - RADIUS :], "lat", 1)
    below = line(both[:RADIUS], "lat", -1)
    extended = jnp.concatenate([above, both, below], axis=0)
    west = ring(extended[:, cols - SIDE :], "lon", 1)
    east = ring(extended[:, :SIDE], "lon", -1)
    place, grads = lax.optimization_barrier((place, grads))
    kv, norm, keep, give = forward(
        place, queries, extended, west, east, up_flat, lat_total, out_rows
    )
    got = lax.ppermute(give, "lon", [(i, i ^ 1) for i in range(lon)])
    grad_query, mid, rim, left, right = backward(
        place, queries, grads, kv, norm, lat_total
    )
    keep, left, right = lax.optimization_barrier((keep, left, right))
    from_east = ring(left, "lon", -1)
    from_west = ring(right, "lon", 1)
    half = pl.pallas_call(
        fold_kernel,
        out_shape=shape(keep.shape),
        compiler_params=SMALL,
        cost_estimate=cost(FOLD),
        name="fold",
    )(keep, got)
    same_core = [[2 * i + c for i in range(lon // 2)] for c in range(2)]
    terms = lax.all_to_all(half, "lon", 0, 0, axis_index_groups=same_core, tiled=True)
    from_west, from_east, _ = lax.optimization_barrier((from_west, from_east, half))
    top, bottom = pl.pallas_call(
        rim_kernel,
        out_shape=(shape((RADIUS, cols, 2 * inner)),) * 2,
        compiler_params=SMALL,
        cost_estimate=cost(RIM),
        name="rim",
    )(rim, from_west, from_east)
    from_below = line(top, "lat", -1)
    from_above = line(bottom, "lat", 1)
    terms, _ = lax.optimization_barrier((terms, top))
    copies = pl.pallas_call(
        share_kernel,
        out_shape=shape((lat, out_rows, model)),
        compiler_params=SMALL,
        name="share",
    )(terms)
    every = lax.all_to_all(copies, "lat", 0, 0, tiled=True)
    from_above, from_below, _ = lax.optimization_barrier((from_above, from_below, copies))
    grad_key, grad_value = pl.pallas_call(
        finish_kernel,
        out_shape=(shape((rows, cols, inner)),) * 2,
        compiler_params=SMALL,
        cost_estimate=cost(FINISH),
        name="finish",
    )(mid, from_west, from_east, from_above, from_below)
    grad_weight = pl.pallas_call(
        functools.partial(mean_kernel, lat_total),
        out_shape=shape((out_rows, model), jnp.float32),
        compiler_params=SMALL,
        name="mean",
    )(every)
    return (grad_query, grad_key, grad_value, grad_weight)


def solution(mesh):
    placed = P("lat", "lon", None)
    return jax.shard_map(
        shards,
        mesh=mesh,
        in_specs=(placed, placed, placed, placed, P()),
        out_specs=(placed, placed, placed, P("lon", None)),
        check_vma=False,
    )
```

```python
import functools

import jax
import jax.numpy as jnp
from jax import lax
from jax.experimental import pallas as pl
from jax.experimental.pallas import tpu as pltpu
from jax.sharding import PartitionSpec as P

HEADS = 8
RADIUS = 6
SIDE = 8
LANES = 128
STRIP = 4
PACK = 4

NT = (((1,), (1,)), ((), ()))
NN = (((1,), (0,)), ((), ()))


def mm(a, b, dims):
    return lax.dot_general(a, b, dims, preferred_element_type=jnp.float32)


def spread(block, diag):
    tall = jnp.concatenate([block.astype(jnp.float32)] * PACK, axis=0)
    return jnp.where(diag, tall, 0.0).astype(jnp.bfloat16)


def diagonal(square, head, strip_q):
    return jnp.concatenate(
        [square[h * head : (h + 1) * head, h * strip_q : (h + 1) * strip_q] for h in range(PACK)],
        axis=0,
    )


def masks(rows, cols, inner):
    head = inner // HEADS
    wide = cols + 2 * SIDE
    strip_q = STRIP * cols
    slab = (STRIP + 2 * RADIUS) * wide
    lanes = PACK * strip_q
    key = lax.broadcasted_iota(jnp.int32, (slab, lanes), 0)
    query = lax.broadcasted_iota(jnp.int32, (slab, lanes), 1) & (strip_q - 1)
    row = key // wide
    place = key & (wide - 1)
    col = jnp.where(
        place < cols, place, jnp.where(place < cols + SIDE, place - cols - SIDE, place - SIDE)
    )
    row_gap = row - query // cols
    col_gap = jnp.abs(col - (query & (cols - 1)))
    near = (row_gap >= 0) & (row_gap <= 2 * RADIUS) & (col_gap <= RADIUS)
    diag = (lax.broadcasted_iota(jnp.int32, (lanes, PACK * head), 0) // strip_q) == (
        lax.broadcasted_iota(jnp.int32, (lanes, PACK * head), 1) // head
    )
    return near, row, diag


def beside(west, east):
    pair = [west.astype(jnp.float32), east.astype(jnp.float32)]
    return jnp.concatenate(pair, axis=1).astype(jnp.bfloat16)


def geometry(rows, cols, inner):
    head = inner // HEADS
    group = PACK * head
    strip_q = STRIP * cols
    slab_rows = STRIP + 2 * RADIUS
    wide = cols + 2 * SIDE
    return head, group, strip_q, slab_rows, wide, slab_rows * wide


def query_kernel(
    lat_total, place_ref, qg_ref, ext_ref, west_ref, east_ref, up_ref,
    dq_ref, stats_ref, keep_ref, give_ref, kv, kt, vt, att_t, dq_t, raw,
):
    rows, cols, inner = dq_ref.shape
    ext_rows = rows + 2 * RADIUS
    head, group, strip_q, slab_rows, wide, slab = geometry(rows, cols, inner)
    scale = head ** (-0.5)
    base, core = place_ref[0], place_ref[1]

    kv[:, 0:cols, :] = ext_ref[...]
    kv[:, cols:wide, :] = beside(west_ref[...], east_ref[...])
    kt[...] = kv[:, :, 0:inner].reshape(ext_rows * wide, inner).T
    vt[...] = kv[:, :, inner:].reshape(ext_rows * wide, inner).T
    near, row, diag = masks(rows, cols, inner)

    for s in range(rows // STRIP):
        first = s * STRIP
        low = RADIUS - base - first
        allowed = near & (row >= low) & (row < low + lat_total)
        window = slice(first * wide, first * wide + slab)
        here = slice(s * strip_q, (s + 1) * strip_q)
        for part in range(HEADS // PACK):
            chans = slice(part * group, (part + 1) * group)
            others = slice(inner + part * group, inner + (part + 1) * group)
            keys = kv[first : first + slab_rows, :, chans].reshape(slab, group)
            values = kv[first : first + slab_rows, :, others].reshape(slab, group)
            q_wide = spread(
                qg_ref[first : first + STRIP, :, chans].reshape(strip_q, group) * scale, diag
            )
            g_wide = spread(qg_ref[first : first + STRIP, :, others].reshape(strip_q, group), diag)
            scores = jnp.where(allowed, mm(keys, q_wide, NT), -1e30)
            top = jnp.max(scores, axis=0, keepdims=True)
            weights = jnp.exp(scores - top)
            total = jnp.sum(weights, axis=0, keepdims=True)
            probs = weights * (1.0 / total)
            low_probs = probs.astype(jnp.bfloat16)
            att_t[chans, here] = diagonal(mm(vt[chans, window], low_probs, NN), head, strip_q)
            grad_prob = mm(values, g_wide, NT)
            delta = jnp.sum(low_probs.astype(jnp.float32) * grad_prob, axis=0, keepdims=True)
            grad_score = (probs * (grad_prob - delta)).astype(jnp.bfloat16)
            dq_t[chans, here] = diagonal(mm(kt[chans, window], grad_score, NN), head, strip_q) * scale
            norm = top + jnp.log(total)
            for h in range(PACK):
                at = part * PACK + h
                own = slice(h * strip_q, (h + 1) * strip_q)
                raw[at : at + 1, here] = norm[:, own]
                raw[HEADS + at : HEADS + at + 1, here] = delta[:, own]

    weight = mm(att_t[...].astype(jnp.bfloat16), up_ref[...], NN)
    weight = weight.reshape(keep_ref.shape[0], 2, keep_ref.shape[1], weight.shape[1])
    keep_ref[...] = jnp.where(core == 0, weight[:, 0], weight[:, 1])
    give_ref[...] = jnp.where(core == 0, weight[:, 1], weight[:, 0]).astype(jnp.bfloat16)
    terms = []
    for kind in range(2):
        rest = raw[kind * HEADS : (kind + 1) * HEADS, :]
        for _ in range(3):
            term = rest.astype(jnp.bfloat16).astype(jnp.float32)
            terms.append(term)
            rest = rest - term
    lanes = stats_ref.shape[2]
    terms.append(jnp.zeros((lanes - 6 * HEADS, rows * cols), jnp.float32))
    table = jnp.concatenate(terms, axis=0)
    stats_ref[...] = table.T.astype(jnp.bfloat16).reshape(rows, cols, lanes)
    dq_ref[...] = dq_t[...].T.astype(jnp.bfloat16).reshape(rows, cols, inner)


def key_kernel(
    lat_total, place_ref, keys_ref, values_ref, q_above, q_own, q_below, s_above, s_own, s_below,
    west_ref, east_ref,
    dk_ref, dv_ref, qg, stats, qt, gt, dk_t, dv_t,
):
    rows, cols, inner = dk_ref.shape
    ext_rows = rows + 2 * RADIUS
    head, group, strip_k, slab_rows, wide, slab = geometry(rows, cols, inner)
    scale = head ** (-0.5)
    lanes = s_own.shape[2]
    base = place_ref[0]

    for at, size, main, extra in (
        (0, RADIUS, q_above, s_above),
        (RADIUS, rows, q_own, s_own),
        (RADIUS + rows, RADIUS, q_below, s_below),
    ):
        qg[at : at + size, 0:cols, :] = main[...]
        stats[at : at + size, 0:cols, :] = extra[...]
    qg[:, cols:wide, :] = beside(west_ref[:, :, 0 : 2 * inner], east_ref[:, :, 0 : 2 * inner])
    stats[:, cols:wide, :] = beside(west_ref[:, :, 2 * inner :], east_ref[:, :, 2 * inner :])
    qt[...] = qg[:, :, 0:inner].reshape(ext_rows * wide, inner).T
    gt[...] = qg[:, :, inner:].reshape(ext_rows * wide, inner).T
    near, row, diag = masks(rows, cols, inner)
    lane = lax.broadcasted_iota(jnp.int32, (lanes, group), 0)
    of_head = lax.broadcasted_iota(jnp.int32, (lanes, group), 1) // strip_k

    def picked(kind, part):
        wanted = ((lane & (HEADS - 1)) == of_head + part * PACK) & (lane // (3 * HEADS) == kind)
        return jnp.where(wanted, 1.0, 0.0).astype(jnp.bfloat16)

    for s in range(rows // STRIP):
        first = s * STRIP
        low = RADIUS - base - first
        allowed = near & (row >= low) & (row < low + lat_total)
        window = slice(first * wide, first * wide + slab)
        here = slice(s * strip_k, (s + 1) * strip_k)
        table = stats[first : first + slab_rows].reshape(slab, lanes)
        for part in range(HEADS // PACK):
            chans = slice(part * group, (part + 1) * group)
            others = slice(inner + part * group, inner + (part + 1) * group)
            queries = qg[first : first + slab_rows, :, chans].reshape(slab, group)
            grads = qg[first : first + slab_rows, :, others].reshape(slab, group)
            k_wide = spread(
                keys_ref[first : first + STRIP, :, chans].reshape(strip_k, group) * scale, diag
            )
            v_wide = spread(values_ref[first : first + STRIP, :, chans].reshape(strip_k, group), diag)
            scores = mm(queries, k_wide, NT) - mm(table, picked(0, part), NN)
            probs = jnp.exp(jnp.where(allowed, scores, -1e30))
            grad_prob = mm(grads, v_wide, NT) - mm(table, picked(1, part), NN)
            grad_score = (probs * grad_prob).astype(jnp.bfloat16)
            dv_t[chans, here] = diagonal(
                mm(gt[chans, window], probs.astype(jnp.bfloat16), NN), head, strip_k
            )
            dk_t[chans, here] = diagonal(mm(qt[chans, window], grad_score, NN), head, strip_k) * scale

    dk_ref[...] = dk_t[...].T.astype(jnp.bfloat16).reshape(rows, cols, inner)
    dv_ref[...] = dv_t[...].T.astype(jnp.bfloat16).reshape(rows, cols, inner)


def edge_kernel(q_above, q_own, q_below, s_above, s_own, s_below, last_ref, first_ref):
    deep, rows = q_above.shape[0], q_own.shape[0]
    cols, chans = q_own.shape[1:]
    for at, size, main, extra in (
        (0, deep, q_above, s_above),
        (deep, rows, q_own, s_own),
        (deep + rows, deep, q_below, s_below),
    ):
        for source, lanes in ((main, slice(0, chans)), (extra, slice(chans, chans + extra.shape[2]))):
            block = source[...].astype(jnp.float32)
            first_ref[at : at + size, :, lanes] = block[:, :SIDE].astype(jnp.bfloat16)
            last_ref[at : at + size, :, lanes] = block[:, cols - SIDE :].astype(jnp.bfloat16)


def share_kernel(parts_ref, copies_ref):
    total = jnp.sum(parts_ref[...].astype(jnp.float32), axis=0).astype(jnp.bfloat16)
    copies_ref[...] = jnp.broadcast_to(total[None], copies_ref.shape)


def pack_kernel(keys_ref, values_ref, both_ref, sems):
    inner = keys_ref.shape[2]
    copies = [
        pltpu.make_async_copy(keys_ref, both_ref.at[:, :, pl.ds(0, inner)], sems.at[0]),
        pltpu.make_async_copy(values_ref, both_ref.at[:, :, pl.ds(inner, inner)], sems.at[1]),
    ]
    for copy in copies:
        copy.start()
    for copy in copies:
        copy.wait()


def fold_kernel(keep_ref, got_ref, half_ref):
    half_ref[...] = (keep_ref[...] + got_ref[...].astype(jnp.float32)).astype(jnp.bfloat16)


def mean_kernel(parts, terms_ref, out_ref):
    out_ref[...] = jnp.sum(terms_ref[...].astype(jnp.float32), axis=0) / parts


VMEM = pl.BlockSpec(memory_space=pltpu.VMEM)
SMEM = pl.BlockSpec(memory_space=pltpu.SMEM)
PARAMS = pltpu.CompilerParams(vmem_limit_bytes=20 << 20)
FOLD, EDGE = 6_000_000_000, 20_000_000_000
QUERY, KEY = 20_000_000_000, 20_000_000_000
SMALL = pltpu.CompilerParams(vmem_limit_bytes=8 << 20)


def shape(dims, kind=jnp.bfloat16):
    return jax.ShapeDtypeStruct(dims, kind)


def cost(flops):
    return pl.CostEstimate(flops=flops, bytes_accessed=4_000_000, transcendentals=0)


def over_queries(place, qg, extended, west, east, upstream, lat_total, out_rows):
    rows, cols = qg.shape[:2]
    inner = qg.shape[2] // 2
    ext_rows, wide = rows + 2 * RADIUS, cols + 2 * SIDE
    model = upstream.shape[1]
    return pl.pallas_call(
        functools.partial(query_kernel, lat_total),
        out_shape=(
            shape((rows, cols, inner)),
            shape((rows, cols, LANES)),
            shape((inner // (2 * out_rows), out_rows, model), jnp.float32),
            shape((inner // (2 * out_rows), out_rows, model)),
        ),
        in_specs=[SMEM] + [VMEM] * 5,
        out_specs=(VMEM,) * 4,
        scratch_shapes=[
            pltpu.VMEM((ext_rows, wide, 2 * inner), jnp.bfloat16),
            pltpu.VMEM((inner, ext_rows * wide), jnp.bfloat16),
            pltpu.VMEM((inner, ext_rows * wide), jnp.bfloat16),
            pltpu.VMEM((inner, rows * cols), jnp.float32),
            pltpu.VMEM((inner, rows * cols), jnp.float32),
            pltpu.VMEM((2 * HEADS, rows * cols), jnp.float32),
        ],
        compiler_params=PARAMS,
        cost_estimate=cost(QUERY),
        name="over_queries",
    )(place, qg, extended, west, east, upstream)


def over_keys(place, keys, values, pieces, west, east, lat_total):
    rows, cols, inner = keys.shape
    ext_rows, wide = rows + 2 * RADIUS, cols + 2 * SIDE
    return pl.pallas_call(
        functools.partial(key_kernel, lat_total),
        out_shape=(shape((rows, cols, inner)),) * 2,
        in_specs=[SMEM] + [VMEM] * 10,
        out_specs=(VMEM,) * 2,
        scratch_shapes=[
            pltpu.VMEM((ext_rows, wide, 2 * inner), jnp.bfloat16),
            pltpu.VMEM((ext_rows, wide, LANES), jnp.bfloat16),
            pltpu.VMEM((inner, ext_rows * wide), jnp.bfloat16),
            pltpu.VMEM((inner, ext_rows * wide), jnp.bfloat16),
            pltpu.VMEM((inner, rows * cols), jnp.float32),
            pltpu.VMEM((inner, rows * cols), jnp.float32),
        ],
        compiler_params=PARAMS,
        cost_estimate=cost(KEY),
        name="over_keys",
    )(place, keys, values, *pieces, west, east)


def ring(block, axis, by):
    size = lax.axis_size(axis)
    return lax.ppermute(block, axis, [(i, (i + by) % size) for i in range(size)])


def line(block, axis, by):
    size = lax.axis_size(axis)
    return lax.ppermute(
        block, axis, [(i, i + by) for i in range(size) if 0 <= i + by < size]
    )


def packed(left, right, name):
    rows, cols, inner = left.shape
    return pl.pallas_call(
        pack_kernel,
        out_shape=shape((rows, cols, 2 * inner)),
        in_specs=[pl.BlockSpec(memory_space=pl.ANY)] * 2,
        out_specs=VMEM,
        scratch_shapes=[pltpu.SemaphoreType.DMA((2,))],
        compiler_params=SMALL,
        name=name,
    )(left, right)


def poles(block):
    above = line(block[block.shape[0] - RADIUS :], "lat", 1)
    below = line(block[:RADIUS], "lat", -1)
    return above, below


def shards(queries, keys, values, upstream, out_weight):
    rows, cols, inner = queries.shape
    model = upstream.shape[2]
    tokens = rows * cols
    lat, lon = lax.axis_size("lat"), lax.axis_size("lon")
    lat_total = rows * lat
    out_rows = inner // lon
    place = jnp.stack([lax.axis_index("lat") * rows, lax.axis_index("lon") % 2]).astype(jnp.int32)
    up_flat = upstream.reshape(tokens, model)
    grads = (
        jnp.einsum("td,id->ti", up_flat, out_weight, preferred_element_type=jnp.float32)
        .astype(jnp.bfloat16)
        .reshape(rows, cols, inner)
    )
    both = packed(keys, values, "pack_kv")
    above, below = poles(both)
    extended = jnp.concatenate([above, both, below], axis=0)
    west = ring(extended[:, cols - SIDE :], "lon", 1)
    east = ring(extended[:, :SIDE], "lon", -1)

    grads, _ = lax.optimization_barrier((grads, extended))
    qg = packed(queries, grads, "pack_qg")
    q_above, q_below = poles(qg)
    grad_query, stats, keep, give = over_queries(
        place, qg, extended, west, east, up_flat, lat_total, out_rows
    )

    got = lax.ppermute(give, "lon", [(i, i ^ 1) for i in range(lon)])
    half = pl.pallas_call(
        fold_kernel,
        out_shape=shape(keep.shape),
        compiler_params=SMALL,
        cost_estimate=cost(FOLD),
        name="fold",
    )(keep, got)
    same_core = [[2 * i + c for i in range(lon // 2)] for c in range(2)]
    terms = lax.all_to_all(half, "lon", 0, 0, axis_index_groups=same_core, tiled=True)

    stats, _ = lax.optimization_barrier((stats, half))
    s_above, s_below = poles(stats)
    q_above, q_below, s_above, s_below = lax.optimization_barrier(
        (q_above, q_below, s_above, s_below)
    )
    pieces = (q_above, qg, q_below, s_above, stats, s_below)
    last, first = pl.pallas_call(
        edge_kernel,
        out_shape=(shape((rows + 2 * RADIUS, SIDE, 2 * inner + LANES)),) * 2,
        compiler_params=SMALL,
        cost_estimate=cost(EDGE),
        name="edge",
    )(*pieces)
    q_west = ring(last, "lon", 1)
    q_east = ring(first, "lon", -1)
    terms, _ = lax.optimization_barrier((terms, first))
    copies = pl.pallas_call(
        share_kernel,
        out_shape=shape((lat, out_rows, model)),
        compiler_params=SMALL,
        name="share",
    )(terms)
    every = lax.all_to_all(copies, "lat", 0, 0, tiled=True)
    q_west, q_east, _ = lax.optimization_barrier((q_west, q_east, copies))
    grad_key, grad_value = over_keys(
        place, keys, values, pieces, q_west, q_east, lat_total
    )
    grad_weight = pl.pallas_call(
        functools.partial(mean_kernel, lat_total),
        out_shape=shape((out_rows, model), jnp.float32),
        compiler_params=SMALL,
        name="mean",
    )(every)
    return (grad_query, grad_key, grad_value, grad_weight)


def solution(mesh):
    placed = P("lat", "lon", None)
    return jax.shard_map(
        shards,
        mesh=mesh,
        in_specs=(placed, placed, placed, placed, P()),
        out_specs=(placed, placed, placed, P("lon", None)),
        check_vma=False,
    )
```

```python
import functools

import jax
import jax.numpy as jnp
from jax import lax
from jax.experimental import pallas as pl
from jax.experimental.pallas import tpu as pltpu
from jax.sharding import PartitionSpec as P

HEADS = 8
RADIUS = 6
SIDE = 8
LANES = 128
STRIP = 4
PACK = 4

NT = (((1,), (1,)), ((), ()))
NN = (((1,), (0,)), ((), ()))


def mm(a, b, dims):
    return lax.dot_general(a, b, dims, preferred_element_type=jnp.float32)


def spread(block, diag):
    tall = jnp.concatenate([block.astype(jnp.float32)] * PACK, axis=0)
    return jnp.where(diag, tall, 0.0).astype(jnp.bfloat16)


def diagonal(square, head, strip_q):
    return jnp.concatenate(
        [square[h * head : (h + 1) * head, h * strip_q : (h + 1) * strip_q] for h in range(PACK)],
        axis=0,
    )


def masks(rows, cols, inner):
    head = inner // HEADS
    wide = cols + 2 * SIDE
    strip_q = STRIP * cols
    slab = (STRIP + 2 * RADIUS) * wide
    lanes = PACK * strip_q
    key = lax.broadcasted_iota(jnp.int32, (slab, lanes), 0)
    query = lax.broadcasted_iota(jnp.int32, (slab, lanes), 1) & (strip_q - 1)
    row = key // wide
    place = key & (wide - 1)
    col = jnp.where(
        place < cols, place, jnp.where(place < cols + SIDE, place - cols - SIDE, place - SIDE)
    )
    row_gap = row - query // cols
    col_gap = jnp.abs(col - (query & (cols - 1)))
    near = (row_gap >= 0) & (row_gap <= 2 * RADIUS) & (col_gap <= RADIUS)
    diag = (lax.broadcasted_iota(jnp.int32, (lanes, PACK * head), 0) // strip_q) == (
        lax.broadcasted_iota(jnp.int32, (lanes, PACK * head), 1) // head
    )
    return near, row, diag


def beside(west, east):
    pair = [west.astype(jnp.float32), east.astype(jnp.float32)]
    return jnp.concatenate(pair, axis=1).astype(jnp.bfloat16)


def geometry(rows, cols, inner):
    head = inner // HEADS
    group = PACK * head
    strip_q = STRIP * cols
    slab_rows = STRIP + 2 * RADIUS
    wide = cols + 2 * SIDE
    return head, group, strip_q, slab_rows, wide, slab_rows * wide


def query_kernel(
    lat_total, place_ref, qg_ref, ext_ref, west_ref, east_ref, up_ref,
    dq_ref, stats_ref, term_ref, kv, kt, vt, att_t, dq_t, raw,
):
    rows, cols, inner = dq_ref.shape
    ext_rows = rows + 2 * RADIUS
    head, group, strip_q, slab_rows, wide, slab = geometry(rows, cols, inner)
    scale = head ** (-0.5)
    base = place_ref[0]

    kv[:, 0:cols, :] = ext_ref[...]
    kv[:, cols:wide, :] = beside(west_ref[...], east_ref[...])
    kt[...] = kv[:, :, 0:inner].reshape(ext_rows * wide, inner).T
    vt[...] = kv[:, :, inner:].reshape(ext_rows * wide, inner).T
    near, row, diag = masks(rows, cols, inner)

    for s in range(rows // STRIP):
        first = s * STRIP
        low = RADIUS - base - first
        allowed = near & (row >= low) & (row < low + lat_total)
        window = slice(first * wide, first * wide + slab)
        here = slice(s * strip_q, (s + 1) * strip_q)
        for part in range(HEADS // PACK):
            chans = slice(part * group, (part + 1) * group)
            others = slice(inner + part * group, inner + (part + 1) * group)
            keys = kv[first : first + slab_rows, :, chans].reshape(slab, group)
            values = kv[first : first + slab_rows, :, others].reshape(slab, group)
            q_wide = spread(
                qg_ref[first : first + STRIP, :, chans].reshape(strip_q, group) * scale, diag
            )
            g_wide = spread(qg_ref[first : first + STRIP, :, others].reshape(strip_q, group), diag)
            scores = jnp.where(allowed, mm(keys, q_wide, NT), -1e30)
            top = jnp.max(scores, axis=0, keepdims=True)
            weights = jnp.exp(scores - top)
            total = jnp.sum(weights, axis=0, keepdims=True)
            probs = weights * (1.0 / total)
            low_probs = probs.astype(jnp.bfloat16)
            att_t[chans, here] = diagonal(mm(vt[chans, window], low_probs, NN), head, strip_q)
            grad_prob = mm(values, g_wide, NT)
            delta = jnp.sum(low_probs.astype(jnp.float32) * grad_prob, axis=0, keepdims=True)
            grad_score = (probs * (grad_prob - delta)).astype(jnp.bfloat16)
            dq_t[chans, here] = diagonal(mm(kt[chans, window], grad_score, NN), head, strip_q) * scale
            norm = top + jnp.log(total)
            for h in range(PACK):
                at = part * PACK + h
                own = slice(h * strip_q, (h + 1) * strip_q)
                raw[at : at + 1, here] = norm[:, own]
                raw[HEADS + at : HEADS + at + 1, here] = delta[:, own]

    weight = mm(att_t[...].astype(jnp.bfloat16), up_ref[...], NN)
    weight = weight.reshape(term_ref.shape[1], 2, term_ref.shape[2], weight.shape[1])
    for core in range(2):
        term_ref[core] = weight[:, core].astype(jnp.bfloat16)
    terms = []
    for kind in range(2):
        rest = raw[kind * HEADS : (kind + 1) * HEADS, :]
        for _ in range(3):
            term = rest.astype(jnp.bfloat16).astype(jnp.float32)
            terms.append(term)
            rest = rest - term
    lanes = stats_ref.shape[2]
    terms.append(jnp.zeros((lanes - 6 * HEADS, rows * cols), jnp.float32))
    table = jnp.concatenate(terms, axis=0)
    stats_ref[...] = table.T.astype(jnp.bfloat16).reshape(rows, cols, lanes)
    dq_ref[...] = dq_t[...].T.astype(jnp.bfloat16).reshape(rows, cols, inner)


def key_kernel(
    lat_total, place_ref, keys_ref, values_ref, q_above, q_own, q_below, s_above, s_own, s_below,
    west_ref, east_ref,
    dk_ref, dv_ref, qg, stats, qt, gt, dk_t, dv_t,
):
    rows, cols, inner = dk_ref.shape
    ext_rows = rows + 2 * RADIUS
    head, group, strip_k, slab_rows, wide, slab = geometry(rows, cols, inner)
    scale = head ** (-0.5)
    lanes = s_own.shape[2]
    base = place_ref[0]

    for at, size, main, extra in (
        (0, RADIUS, q_above, s_above),
        (RADIUS, rows, q_own, s_own),
        (RADIUS + rows, RADIUS, q_below, s_below),
    ):
        qg[at : at + size, 0:cols, :] = main[...]
        stats[at : at + size, 0:cols, :] = extra[...]
    qg[:, cols:wide, :] = beside(west_ref[:, :, 0 : 2 * inner], east_ref[:, :, 0 : 2 * inner])
    stats[:, cols:wide, :] = beside(west_ref[:, :, 2 * inner :], east_ref[:, :, 2 * inner :])
    qt[...] = qg[:, :, 0:inner].reshape(ext_rows * wide, inner).T
    gt[...] = qg[:, :, inner:].reshape(ext_rows * wide, inner).T
    near, row, diag = masks(rows, cols, inner)
    lane = lax.broadcasted_iota(jnp.int32, (lanes, group), 0)
    of_head = lax.broadcasted_iota(jnp.int32, (lanes, group), 1) // strip_k

    def picked(kind, part):
        wanted = ((lane & (HEADS - 1)) == of_head + part * PACK) & (lane // (3 * HEADS) == kind)
        return jnp.where(wanted, 1.0, 0.0).astype(jnp.bfloat16)

    for s in range(rows // STRIP):
        first = s * STRIP
        low = RADIUS - base - first
        allowed = near & (row >= low) & (row < low + lat_total)
        window = slice(first * wide, first * wide + slab)
        here = slice(s * strip_k, (s + 1) * strip_k)
        table = stats[first : first + slab_rows].reshape(slab, lanes)
        for part in range(HEADS // PACK):
            chans = slice(part * group, (part + 1) * group)
            others = slice(inner + part * group, inner + (part + 1) * group)
            queries = qg[first : first + slab_rows, :, chans].reshape(slab, group)
            grads = qg[first : first + slab_rows, :, others].reshape(slab, group)
            k_wide = spread(
                keys_ref[first : first + STRIP, :, chans].reshape(strip_k, group) * scale, diag
            )
            v_wide = spread(values_ref[first : first + STRIP, :, chans].reshape(strip_k, group), diag)
            scores = mm(queries, k_wide, NT) - mm(table, picked(0, part), NN)
            probs = jnp.exp(jnp.where(allowed, scores, -1e30))
            grad_prob = mm(grads, v_wide, NT) - mm(table, picked(1, part), NN)
            grad_score = (probs * grad_prob).astype(jnp.bfloat16)
            dv_t[chans, here] = diagonal(
                mm(gt[chans, window], probs.astype(jnp.bfloat16), NN), head, strip_k
            )
            dk_t[chans, here] = diagonal(mm(qt[chans, window], grad_score, NN), head, strip_k) * scale

    dk_ref[...] = dk_t[...].T.astype(jnp.bfloat16).reshape(rows, cols, inner)
    dv_ref[...] = dv_t[...].T.astype(jnp.bfloat16).reshape(rows, cols, inner)


def edge_kernel(q_above, q_own, q_below, s_above, s_own, s_below, last_ref, first_ref):
    deep, rows = q_above.shape[0], q_own.shape[0]
    cols, chans = q_own.shape[1:]
    for at, size, main, extra in (
        (0, deep, q_above, s_above),
        (deep, rows, q_own, s_own),
        (deep + rows, deep, q_below, s_below),
    ):
        for source, lanes in ((main, slice(0, chans)), (extra, slice(chans, chans + extra.shape[2]))):
            block = source[...].astype(jnp.float32)
            first_ref[at : at + size, :, lanes] = block[:, :SIDE].astype(jnp.bfloat16)
            last_ref[at : at + size, :, lanes] = block[:, cols - SIDE :].astype(jnp.bfloat16)


def share_kernel(parts_ref, copies_ref):
    total = jnp.sum(parts_ref[...].astype(jnp.float32), axis=0).astype(jnp.bfloat16)
    copies_ref[...] = jnp.broadcast_to(total[None], copies_ref.shape)


def pack_kernel(keys_ref, values_ref, both_ref, sems):
    inner = keys_ref.shape[2]
    copies = [
        pltpu.make_async_copy(keys_ref, both_ref.at[:, :, pl.ds(0, inner)], sems.at[0]),
        pltpu.make_async_copy(values_ref, both_ref.at[:, :, pl.ds(inner, inner)], sems.at[1]),
    ]
    for copy in copies:
        copy.start()
    for copy in copies:
        copy.wait()


def fold_kernel(pair_ref, half_ref):
    pair = pair_ref[...].astype(jnp.float32)
    half_ref[...] = (pair[0] + pair[1]).astype(jnp.bfloat16)


def mean_kernel(parts, terms_ref, out_ref):
    out_ref[...] = jnp.sum(terms_ref[...].astype(jnp.float32), axis=0) / parts


VMEM = pl.BlockSpec(memory_space=pltpu.VMEM)
SMEM = pl.BlockSpec(memory_space=pltpu.SMEM)
PARAMS = pltpu.CompilerParams(vmem_limit_bytes=20 << 20)
FOLD, EDGE = 1_000_000, 4_000_000_000
QUERY, KEY = 40_000_000_000, 20_000_000_000
SMALL = pltpu.CompilerParams(vmem_limit_bytes=8 << 20)


def shape(dims, kind=jnp.bfloat16):
    return jax.ShapeDtypeStruct(dims, kind)


def cost(flops):
    return pl.CostEstimate(flops=flops, bytes_accessed=4_000_000, transcendentals=0)


def over_queries(place, qg, extended, west, east, upstream, lat_total, out_rows):
    rows, cols = qg.shape[:2]
    inner = qg.shape[2] // 2
    ext_rows, wide = rows + 2 * RADIUS, cols + 2 * SIDE
    model = upstream.shape[1]
    return pl.pallas_call(
        functools.partial(query_kernel, lat_total),
        out_shape=(
            shape((rows, cols, inner)),
            shape((rows, cols, LANES)),
            shape((2, inner // (2 * out_rows), out_rows, model)),
        ),
        in_specs=[SMEM] + [VMEM] * 5,
        out_specs=(VMEM,) * 3,
        scratch_shapes=[
            pltpu.VMEM((ext_rows, wide, 2 * inner), jnp.bfloat16),
            pltpu.VMEM((inner, ext_rows * wide), jnp.bfloat16),
            pltpu.VMEM((inner, ext_rows * wide), jnp.bfloat16),
            pltpu.VMEM((inner, rows * cols), jnp.float32),
            pltpu.VMEM((inner, rows * cols), jnp.float32),
            pltpu.VMEM((2 * HEADS, rows * cols), jnp.float32),
        ],
        compiler_params=PARAMS,
        cost_estimate=cost(QUERY),
        name="over_queries",
    )(place, qg, extended, west, east, upstream)


def over_keys(place, keys, values, pieces, west, east, lat_total):
    rows, cols, inner = keys.shape
    ext_rows, wide = rows + 2 * RADIUS, cols + 2 * SIDE
    return pl.pallas_call(
        functools.partial(key_kernel, lat_total),
        out_shape=(shape((rows, cols, inner)),) * 2,
        in_specs=[SMEM] + [VMEM] * 10,
        out_specs=(VMEM,) * 2,
        scratch_shapes=[
            pltpu.VMEM((ext_rows, wide, 2 * inner), jnp.bfloat16),
            pltpu.VMEM((ext_rows, wide, LANES), jnp.bfloat16),
            pltpu.VMEM((inner, ext_rows * wide), jnp.bfloat16),
            pltpu.VMEM((inner, ext_rows * wide), jnp.bfloat16),
            pltpu.VMEM((inner, rows * cols), jnp.float32),
            pltpu.VMEM((inner, rows * cols), jnp.float32),
        ],
        compiler_params=PARAMS,
        cost_estimate=cost(KEY),
        name="over_keys",
    )(place, keys, values, *pieces, west, east)


def ring(block, axis, by):
    size = lax.axis_size(axis)
    return lax.ppermute(block, axis, [(i, (i + by) % size) for i in range(size)])


def line(block, axis, by):
    size = lax.axis_size(axis)
    return lax.ppermute(
        block, axis, [(i, i + by) for i in range(size) if 0 <= i + by < size]
    )


def packed(left, right, name):
    rows, cols, inner = left.shape
    return pl.pallas_call(
        pack_kernel,
        out_shape=shape((rows, cols, 2 * inner)),
        in_specs=[pl.BlockSpec(memory_space=pl.ANY)] * 2,
        out_specs=VMEM,
        scratch_shapes=[pltpu.SemaphoreType.DMA((2,))],
        compiler_params=SMALL,
        name=name,
    )(left, right)


def poles(block):
    above = line(block[block.shape[0] - RADIUS :], "lat", 1)
    below = line(block[:RADIUS], "lat", -1)
    return above, below


def shards(queries, keys, values, upstream, out_weight):
    rows, cols, inner = queries.shape
    model = upstream.shape[2]
    tokens = rows * cols
    lat, lon = lax.axis_size("lat"), lax.axis_size("lon")
    lat_total = rows * lat
    out_rows = inner // lon
    place = (lax.axis_index("lat") * rows).astype(jnp.int32).reshape(1)
    up_flat = upstream.reshape(tokens, model)
    grads = (
        jnp.einsum("td,id->ti", up_flat, out_weight, preferred_element_type=jnp.float32)
        .astype(jnp.bfloat16)
        .reshape(rows, cols, inner)
    )
    both = packed(keys, values, "pack_kv")
    above, below = poles(both)
    extended = jnp.concatenate([above, both, below], axis=0)
    west = ring(extended[:, cols - SIDE :], "lon", 1)
    east = ring(extended[:, :SIDE], "lon", -1)

    grads, _ = lax.optimization_barrier((grads, extended))
    qg = packed(queries, grads, "pack_qg")
    q_above, q_below = poles(qg)
    grad_query, stats, term = over_queries(
        place, qg, extended, west, east, up_flat, lat_total, out_rows
    )

    chips = [[2 * i, 2 * i + 1] for i in range(lon // 2)]
    pair = lax.all_to_all(term, "lon", 0, 0, axis_index_groups=chips, tiled=True)
    half = pl.pallas_call(
        fold_kernel,
        out_shape=shape(term.shape[1:]),
        compiler_params=SMALL,
        cost_estimate=cost(FOLD),
        name="fold",
    )(pair)
    same_core = [[2 * i + c for i in range(lon // 2)] for c in range(2)]
    terms = lax.all_to_all(half, "lon", 0, 0, axis_index_groups=same_core, tiled=True)

    stats, _ = lax.optimization_barrier((stats, half))
    s_above, s_below = poles(stats)
    q_above, q_below, s_above, s_below = lax.optimization_barrier(
        (q_above, q_below, s_above, s_below)
    )
    pieces = (q_above, qg, q_below, s_above, stats, s_below)
    last, first = pl.pallas_call(
        edge_kernel,
        out_shape=(shape((rows + 2 * RADIUS, SIDE, 2 * inner + LANES)),) * 2,
        compiler_params=SMALL,
        cost_estimate=cost(EDGE),
        name="edge",
    )(*pieces)
    q_west = ring(last, "lon", 1)
    q_east = ring(first, "lon", -1)
    terms, _ = lax.optimization_barrier((terms, first))
    copies = pl.pallas_call(
        share_kernel,
        out_shape=shape((lat, out_rows, model)),
        compiler_params=SMALL,
        name="share",
    )(terms)
    every = lax.all_to_all(copies, "lat", 0, 0, tiled=True)
    q_west, q_east, _ = lax.optimization_barrier((q_west, q_east, copies))
    grad_key, grad_value = over_keys(
        place, keys, values, pieces, q_west, q_east, lat_total
    )
    grad_weight = pl.pallas_call(
        functools.partial(mean_kernel, lat_total),
        out_shape=shape((out_rows, model), jnp.float32),
        compiler_params=SMALL,
        name="mean",
    )(every)
    return (grad_query, grad_key, grad_value, grad_weight)


def solution(mesh):
    placed = P("lat", "lon", None)
    return jax.shard_map(
        shards,
        mesh=mesh,
        in_specs=(placed, placed, placed, placed, P()),
        out_specs=(placed, placed, placed, P("lon", None)),
        check_vma=False,
    )
```

```python
import functools

import jax
import jax.numpy as jnp
from jax import lax
from jax.experimental import pallas as pl
from jax.experimental.pallas import tpu as pltpu
from jax.sharding import PartitionSpec as P

HEADS = 8
RADIUS = 6
SIDE = 8
STRIP = 4
PACK = 4

NT = (((1,), (1,)), ((), ()))
NN = (((1,), (0,)), ((), ()))


def mm(a, b, dims):
    return lax.dot_general(a, b, dims, preferred_element_type=jnp.float32)


def spread(block, diag):
    tall = jnp.concatenate([block.astype(jnp.float32)] * PACK, axis=0)
    return jnp.where(diag, tall, 0.0).astype(jnp.bfloat16)


def diagonal(square, head, strip_q):
    return jnp.concatenate(
        [square[h * head : (h + 1) * head, h * strip_q : (h + 1) * strip_q] for h in range(PACK)],
        axis=0,
    )


def masks(rows, cols, inner):
    head = inner // HEADS
    wide = cols + 2 * SIDE
    strip_q = STRIP * cols
    slab = (STRIP + 2 * RADIUS) * wide
    lanes = PACK * strip_q
    key = lax.broadcasted_iota(jnp.int32, (slab, lanes), 0)
    query = lax.broadcasted_iota(jnp.int32, (slab, lanes), 1) & (strip_q - 1)
    row = key // wide
    place = key & (wide - 1)
    col = jnp.where(
        place < cols, place, jnp.where(place < cols + SIDE, place - cols - SIDE, place - SIDE)
    )
    row_gap = row - query // cols
    col_gap = jnp.abs(col - (query & (cols - 1)))
    near = (row_gap >= 0) & (row_gap <= 2 * RADIUS) & (col_gap <= RADIUS)
    diag = (lax.broadcasted_iota(jnp.int32, (lanes, PACK * head), 0) // strip_q) == (
        lax.broadcasted_iota(jnp.int32, (lanes, PACK * head), 1) // head
    )
    return near, row, diag


def forward_kernel(
    lat_total, place_ref, q_ref, ext_ref, west_ref, east_ref, up_ref,
    kv_ref, norm_ref, keep_ref, give_ref, vt, att_t,
):
    rows, cols, inner = q_ref.shape
    ext_rows = rows + 2 * RADIUS
    wide = cols + 2 * SIDE
    head = inner // HEADS
    scale = head ** (-0.5)
    group = PACK * head
    strip_q = STRIP * cols
    slab_rows = STRIP + 2 * RADIUS
    slab = slab_rows * wide
    base, core = place_ref[0], place_ref[1]

    kv_ref[:, 0:cols, :] = ext_ref[...]
    kv_ref[:, cols:wide, :] = jnp.concatenate(
        [west_ref[...].astype(jnp.float32), east_ref[...].astype(jnp.float32)], axis=1
    ).astype(jnp.bfloat16)
    vt[...] = kv_ref[:, :, inner:].reshape(ext_rows * wide, inner).T
    near, row, diag = masks(rows, cols, inner)

    for s in range(rows // STRIP):
        first = s * STRIP
        low = RADIUS - base - first
        allowed = near & (row >= low) & (row < low + lat_total)
        window = slice(first * wide, first * wide + slab)
        here = slice(s * strip_q, (s + 1) * strip_q)
        for part in range(HEADS // PACK):
            chans = slice(part * group, (part + 1) * group)
            keys = kv_ref[first : first + slab_rows, :, chans].reshape(slab, group)
            q_wide = spread(
                q_ref[first : first + STRIP, :, chans].reshape(strip_q, group) * scale, diag
            )
            scores = jnp.where(allowed, mm(keys, q_wide, NT), -1e30)
            top = jnp.max(scores, axis=0, keepdims=True)
            weights = jnp.exp(scores - top)
            total = jnp.sum(weights, axis=0, keepdims=True)
            probs = (weights * (1.0 / total)).astype(jnp.bfloat16)
            at = s * (HEADS // PACK) + part
            norm_ref[at : at + 1, :] = top + jnp.log(total)
            att_t[chans, here] = diagonal(mm(vt[chans, window], probs, NN), head, strip_q)

    weight = mm(att_t[...].astype(jnp.bfloat16), up_ref[...], NN)
    out_rows = keep_ref.shape[1]
    weight = weight.reshape(keep_ref.shape[0], 2, out_rows, weight.shape[1])
    keep_ref[...] = jnp.where(core == 0, weight[:, 0], weight[:, 1])
    give_ref[...] = jnp.where(core == 0, weight[:, 1], weight[:, 0]).astype(jnp.bfloat16)


def backward_kernel(
    lat_total, place_ref, q_ref, g_ref, kv_ref, norm_ref,
    dq_ref, mid_ref, rim_ref, left_ref, right_ref, kt, acc, dq_t,
):
    rows, cols, inner = q_ref.shape
    ext_rows = rows + 2 * RADIUS
    wide = cols + 2 * SIDE
    head = inner // HEADS
    scale = head ** (-0.5)
    group = PACK * head
    strip_q = STRIP * cols
    slab_rows = STRIP + 2 * RADIUS
    slab = slab_rows * wide
    base = place_ref[0]

    kt[...] = kv_ref[:, :, 0:inner].reshape(ext_rows * wide, inner).T
    acc[...] = jnp.zeros_like(acc)
    near, row, diag = masks(rows, cols, inner)

    for s in range(rows // STRIP):
        first = s * STRIP
        low = RADIUS - base - first
        allowed = near & (row >= low) & (row < low + lat_total)
        window = slice(first * wide, first * wide + slab)
        here = slice(s * strip_q, (s + 1) * strip_q)
        for part in range(HEADS // PACK):
            chans = slice(part * group, (part + 1) * group)
            vchans = slice(inner + part * group, inner + (part + 1) * group)
            keys = kv_ref[first : first + slab_rows, :, chans].reshape(slab, group)
            values = kv_ref[first : first + slab_rows, :, vchans].reshape(slab, group)
            q_wide = spread(
                q_ref[first : first + STRIP, :, chans].reshape(strip_q, group) * scale, diag
            )
            g_wide = spread(g_ref[first : first + STRIP, :, chans].reshape(strip_q, group), diag)
            at = s * (HEADS // PACK) + part
            scores = jnp.where(allowed, mm(keys, q_wide, NT), -1e30)
            probs = jnp.exp(scores - norm_ref[at : at + 1, :])
            low_probs = probs.astype(jnp.bfloat16)
            grad_prob = mm(values, g_wide, NT)
            delta = jnp.sum(low_probs.astype(jnp.float32) * grad_prob, axis=0, keepdims=True)
            grad_score = (probs * (grad_prob - delta)).astype(jnp.bfloat16)
            dq_t[chans, here] = diagonal(mm(kt[chans, window], grad_score, NN), head, strip_q) * scale
            acc[first : first + slab_rows, :, chans] += mm(grad_score, q_wide, NN).reshape(
                slab_rows, wide, group
            )
            acc[first : first + slab_rows, :, vchans] += mm(low_probs, g_wide, NN).reshape(
                slab_rows, wide, group
            )

    left_ref[...] = acc[:, cols : cols + SIDE, :].astype(jnp.bfloat16)
    right_ref[...] = acc[:, cols + SIDE : wide, :].astype(jnp.bfloat16)
    rim_ref[0:RADIUS] = acc[0:RADIUS, 0:cols, :].astype(jnp.bfloat16)
    rim_ref[RADIUS:] = acc[RADIUS + rows :, 0:cols, :].astype(jnp.bfloat16)
    mid_ref[...] = acc[RADIUS : RADIUS + rows, 0:cols, :].astype(jnp.bfloat16)
    dq_ref[...] = dq_t[...].T.astype(jnp.bfloat16).reshape(rows, cols, inner)


def share_kernel(parts_ref, copies_ref):
    total = jnp.sum(parts_ref[...].astype(jnp.float32), axis=0).astype(jnp.bfloat16)
    copies_ref[...] = jnp.broadcast_to(total[None], copies_ref.shape)


def pack_kernel(keys_ref, values_ref, both_ref, sems):
    inner = keys_ref.shape[2]
    copies = [
        pltpu.make_async_copy(keys_ref, both_ref.at[:, :, pl.ds(0, inner)], sems.at[0]),
        pltpu.make_async_copy(values_ref, both_ref.at[:, :, pl.ds(inner, inner)], sems.at[1]),
    ]
    for copy in copies:
        copy.start()
    for copy in copies:
        copy.wait()


def fold_kernel(keep_ref, got_ref, half_ref):
    half_ref[...] = (keep_ref[...] + got_ref[...].astype(jnp.float32)).astype(jnp.bfloat16)


def mean_kernel(parts, terms_ref, out_ref):
    out_ref[...] = jnp.sum(terms_ref[...].astype(jnp.float32), axis=0) / parts


def wide(block):
    return block.astype(jnp.float32)


def rim_kernel(rim_ref, west_ref, east_ref, top_ref, bottom_ref):
    deep = top_ref.shape[0]
    for out, at, there in (
        (top_ref, 0, 0),
        (bottom_ref, deep, west_ref.shape[0] - deep),
    ):
        side = jnp.concatenate(
            [wide(west_ref[there : there + deep]), wide(east_ref[there : there + deep])], axis=1
        )
        out[...] = (wide(rim_ref[at : at + deep]) + side).astype(jnp.bfloat16)


def finish_kernel(
    mid_ref, west_ref, east_ref, above_ref, below_ref, keys_ref, values_ref
):
    inner = keys_ref.shape[2]
    deep = above_ref.shape[0]
    for out, chans in ((keys_ref, slice(0, inner)), (values_ref, slice(inner, 2 * inner))):
        for at, pole in ((0, above_ref), (deep, below_ref)):
            there = slice(deep + at, 2 * deep + at)
            side = jnp.concatenate(
                [wide(west_ref[there, :, chans]), wide(east_ref[there, :, chans])], axis=1
            )
            total = wide(mid_ref[at : at + deep, :, chans]) + side + wide(pole[:, :, chans])
            out[at : at + deep] = total.astype(jnp.bfloat16)


VMEM = pl.BlockSpec(memory_space=pltpu.VMEM)
SMEM = pl.BlockSpec(memory_space=pltpu.SMEM)
PARAMS = pltpu.CompilerParams(vmem_limit_bytes=20 << 20)
FOLD, RIM, FINISH = 1_000_000, 1_000_000, 3_000_000_000
SMALL = pltpu.CompilerParams(vmem_limit_bytes=8 << 20)


def shape(dims, kind=jnp.bfloat16):
    return jax.ShapeDtypeStruct(dims, kind)


def forward(place, queries, extended, west, east, upstream, lat_total, out_rows):
    rows, cols, inner = queries.shape
    ext_rows, wide = rows + 2 * RADIUS, cols + 2 * SIDE
    model = upstream.shape[1]
    return pl.pallas_call(
        functools.partial(forward_kernel, lat_total),
        out_shape=(
            shape((ext_rows, wide, 2 * inner)),
            shape((8, PACK * STRIP * cols), jnp.float32),
            shape((inner // (2 * out_rows), out_rows, model), jnp.float32),
            shape((inner // (2 * out_rows), out_rows, model)),
        ),
        in_specs=[SMEM] + [VMEM] * 5,
        out_specs=(VMEM,) * 4,
        scratch_shapes=[
            pltpu.VMEM((inner, ext_rows * wide), jnp.bfloat16),
            pltpu.VMEM((inner, rows * cols), jnp.float32),
        ],
        compiler_params=PARAMS,
        cost_estimate=pl.CostEstimate(
            flops=1_000_000_000, bytes_accessed=5_000_000, transcendentals=800_000
        ),
        name="forward",
    )(place, queries, extended, west, east, upstream)


def backward(place, queries, grads, kv, norm, lat_total):
    rows, cols, inner = queries.shape
    ext_rows, wide = rows + 2 * RADIUS, cols + 2 * SIDE
    return pl.pallas_call(
        functools.partial(backward_kernel, lat_total),
        out_shape=(
            shape((rows, cols, inner)),
            shape((rows, cols, 2 * inner)),
            shape((2 * RADIUS, cols, 2 * inner)),
            shape((ext_rows, SIDE, 2 * inner)),
            shape((ext_rows, SIDE, 2 * inner)),
        ),
        in_specs=[SMEM] + [VMEM] * 4,
        out_specs=(VMEM,) * 5,
        scratch_shapes=[
            pltpu.VMEM((inner, ext_rows * wide), jnp.bfloat16),
            pltpu.VMEM((ext_rows, wide, 2 * inner), jnp.float32),
            pltpu.VMEM((inner, rows * cols), jnp.float32),
        ],
        compiler_params=PARAMS,
        cost_estimate=pl.CostEstimate(
            flops=20_000_000_000, bytes_accessed=70_000_000, transcendentals=800_000
        ),
        name="backward",
    )(place, queries, grads, kv, norm)


def ring(block, axis, by):
    size = lax.axis_size(axis)
    return lax.ppermute(block, axis, [(i, (i + by) % size) for i in range(size)])


def line(block, axis, by):
    size = lax.axis_size(axis)
    return lax.ppermute(
        block, axis, [(i, i + by) for i in range(size) if 0 <= i + by < size]
    )


def cost(flops):
    return pl.CostEstimate(flops=flops, bytes_accessed=4_000_000, transcendentals=0)


def shards(queries, keys, values, upstream, out_weight):
    rows, cols, inner = queries.shape
    model = upstream.shape[2]
    tokens = rows * cols
    lat, lon = lax.axis_size("lat"), lax.axis_size("lon")
    lat_total = rows * lat
    out_rows = inner // lon
    place = jnp.stack([lax.axis_index("lat") * rows, lax.axis_index("lon") % 2]).astype(jnp.int32)
    up_flat = upstream.reshape(tokens, model)
    grads = (
        jnp.einsum("td,id->ti", up_flat, out_weight, preferred_element_type=jnp.float32)
        .astype(jnp.bfloat16)
        .reshape(rows, cols, inner)
    )
    both = pl.pallas_call(
        pack_kernel,
        out_shape=shape((rows, cols, 2 * inner)),
        in_specs=[pl.BlockSpec(memory_space=pl.ANY)] * 2,
        out_specs=VMEM,
        scratch_shapes=[pltpu.SemaphoreType.DMA((2,))],
        compiler_params=SMALL,
        name="pack",
    )(keys, values)
    above = line(both[rows - RADIUS :], "lat", 1)
    below = line(both[:RADIUS], "lat", -1)
    extended = jnp.concatenate([above, both, below], axis=0)
    west = ring(extended[:, cols - SIDE :], "lon", 1)
    east = ring(extended[:, :SIDE], "lon", -1)
    place, grads = lax.optimization_barrier((place, grads))
    kv, norm, keep, give = forward(
        place, queries, extended, west, east, up_flat, lat_total, out_rows
    )
    got = lax.ppermute(give, "lon", [(i, i ^ 1) for i in range(lon)])
    grad_query, mid, rim, left, right = backward(
        place, queries, grads, kv, norm, lat_total
    )
    keep, left, right = lax.optimization_barrier((keep, left, right))
    from_east = ring(left, "lon", -1)
    from_west = ring(right, "lon", 1)
    half = pl.pallas_call(
        fold_kernel,
        out_shape=shape(keep.shape),
        compiler_params=SMALL,
        cost_estimate=cost(FOLD),
        name="fold",
    )(keep, got)
    same_core = [[2 * i + c for i in range(lon // 2)] for c in range(2)]
    terms = lax.all_to_all(half, "lon", 0, 0, axis_index_groups=same_core, tiled=True)
    rim, _ = lax.optimization_barrier((rim, half))
    top, bottom = pl.pallas_call(
        rim_kernel,
        out_shape=(shape((RADIUS, cols, 2 * inner)),) * 2,
        compiler_params=SMALL,
        cost_estimate=cost(RIM),
        name="rim",
    )(rim, from_west, from_east)
    from_below = line(top, "lat", -1)
    from_above = line(bottom, "lat", 1)
    terms, _ = lax.optimization_barrier((terms, top))
    copies = pl.pallas_call(
        share_kernel,
        out_shape=shape((lat, out_rows, model)),
        compiler_params=SMALL,
        name="share",
    )(terms)
    every = lax.all_to_all(copies, "lat", 0, 0, tiled=True)
    mid, _ = lax.optimization_barrier((mid, copies))
    grad_key, grad_value = pl.pallas_call(
        finish_kernel,
        out_shape=(shape((rows, cols, inner)),) * 2,
        compiler_params=SMALL,
        cost_estimate=cost(FINISH),
        name="finish",
    )(mid, from_west, from_east, from_above, from_below)
    grad_weight = pl.pallas_call(
        functools.partial(mean_kernel, lat_total),
        out_shape=shape((out_rows, model), jnp.float32),
        compiler_params=SMALL,
        name="mean",
    )(every)
    return (grad_query, grad_key, grad_value, grad_weight)


def solution(mesh):
    placed = P("lat", "lon", None)
    return jax.shard_map(
        shards,
        mesh=mesh,
        in_specs=(placed, placed, placed, placed, P()),
        out_specs=(placed, placed, placed, P("lon", None)),
        check_vma=False,
    )
```

```python
import functools

import jax
import jax.numpy as jnp
from jax import lax
from jax.experimental import pallas as pl
from jax.experimental.pallas import tpu as pltpu
from jax.sharding import PartitionSpec as P

HEADS = 8
RADIUS = 6
SIDE = 8
STRIP = 4
PACK = 4

NT = (((1,), (1,)), ((), ()))
NN = (((1,), (0,)), ((), ()))


def mm(a, b, dims):
    return lax.dot_general(a, b, dims, preferred_element_type=jnp.float32)


def spread(block, diag):
    tall = jnp.concatenate([block.astype(jnp.float32)] * PACK, axis=0)
    return jnp.where(diag, tall, 0.0).astype(jnp.bfloat16)


def diagonal(square, head, strip_q):
    return jnp.concatenate(
        [square[h * head : (h + 1) * head, h * strip_q : (h + 1) * strip_q] for h in range(PACK)],
        axis=0,
    )


def masks(rows, cols, inner):
    head = inner // HEADS
    wide = cols + 2 * SIDE
    strip_q = STRIP * cols
    slab = (STRIP + 2 * RADIUS) * wide
    lanes = PACK * strip_q
    key = lax.broadcasted_iota(jnp.int32, (slab, lanes), 0)
    query = lax.broadcasted_iota(jnp.int32, (slab, lanes), 1) & (strip_q - 1)
    row = key // wide
    place = key & (wide - 1)
    col = jnp.where(
        place < cols, place, jnp.where(place < cols + SIDE, place - cols - SIDE, place - SIDE)
    )
    row_gap = row - query // cols
    col_gap = jnp.abs(col - (query & (cols - 1)))
    near = (row_gap >= 0) & (row_gap <= 2 * RADIUS) & (col_gap <= RADIUS)
    diag = (lax.broadcasted_iota(jnp.int32, (lanes, PACK * head), 0) // strip_q) == (
        lax.broadcasted_iota(jnp.int32, (lanes, PACK * head), 1) // head
    )
    return near, row, diag


def forward_kernel(
    lat_total, place_ref, q_ref, ext_ref, west_ref, east_ref, up_ref,
    kv_ref, norm_ref, keep_ref, give_ref, vt, att_t,
):
    rows, cols, inner = q_ref.shape
    ext_rows = rows + 2 * RADIUS
    wide = cols + 2 * SIDE
    head = inner // HEADS
    scale = head ** (-0.5)
    group = PACK * head
    strip_q = STRIP * cols
    slab_rows = STRIP + 2 * RADIUS
    slab = slab_rows * wide
    base, core = place_ref[0], place_ref[1]

    kv_ref[:, 0:cols, :] = ext_ref[...]
    kv_ref[:, cols:wide, :] = jnp.concatenate(
        [west_ref[...].astype(jnp.float32), east_ref[...].astype(jnp.float32)], axis=1
    ).astype(jnp.bfloat16)
    vt[...] = kv_ref[:, :, inner:].reshape(ext_rows * wide, inner).T
    near, row, diag = masks(rows, cols, inner)

    for s in range(rows // STRIP):
        first = s * STRIP
        low = RADIUS - base - first
        allowed = near & (row >= low) & (row < low + lat_total)
        window = slice(first * wide, first * wide + slab)
        here = slice(s * strip_q, (s + 1) * strip_q)
        for part in range(HEADS // PACK):
            chans = slice(part * group, (part + 1) * group)
            keys = kv_ref[first : first + slab_rows, :, chans].reshape(slab, group)
            q_wide = spread(
                q_ref[first : first + STRIP, :, chans].reshape(strip_q, group) * scale, diag
            )
            scores = jnp.where(allowed, mm(keys, q_wide, NT), -1e30)
            top = jnp.max(scores, axis=0, keepdims=True)
            weights = jnp.exp(scores - top)
            total = jnp.sum(weights, axis=0, keepdims=True)
            probs = (weights * (1.0 / total)).astype(jnp.bfloat16)
            at = s * (HEADS // PACK) + part
            norm_ref[at : at + 1, :] = top + jnp.log(total)
            att_t[chans, here] = diagonal(mm(vt[chans, window], probs, NN), head, strip_q)

    weight = mm(att_t[...].astype(jnp.bfloat16), up_ref[...], NN)
    out_rows = keep_ref.shape[1]
    weight = weight.reshape(keep_ref.shape[0], 2, out_rows, weight.shape[1])
    keep_ref[...] = jnp.where(core == 0, weight[:, 0], weight[:, 1])
    give_ref[...] = jnp.where(core == 0, weight[:, 1], weight[:, 0]).astype(jnp.bfloat16)


def backward_kernel(
    lat_total, place_ref, q_ref, g_ref, kv_ref, norm_ref,
    dq_ref, mid_ref, rim_ref, left_ref, right_ref, kt, acc, dq_t,
):
    rows, cols, inner = q_ref.shape
    ext_rows = rows + 2 * RADIUS
    wide = cols + 2 * SIDE
    head = inner // HEADS
    scale = head ** (-0.5)
    group = PACK * head
    strip_q = STRIP * cols
    slab_rows = STRIP + 2 * RADIUS
    slab = slab_rows * wide
    base = place_ref[0]

    kt[...] = kv_ref[:, :, 0:inner].reshape(ext_rows * wide, inner).T
    acc[...] = jnp.zeros_like(acc)
    near, row, diag = masks(rows, cols, inner)

    for s in range(rows // STRIP):
        first = s * STRIP
        low = RADIUS - base - first
        allowed = near & (row >= low) & (row < low + lat_total)
        window = slice(first * wide, first * wide + slab)
        here = slice(s * strip_q, (s + 1) * strip_q)
        for part in range(HEADS // PACK):
            chans = slice(part * group, (part + 1) * group)
            vchans = slice(inner + part * group, inner + (part + 1) * group)
            keys = kv_ref[first : first + slab_rows, :, chans].reshape(slab, group)
            values = kv_ref[first : first + slab_rows, :, vchans].reshape(slab, group)
            q_wide = spread(
                q_ref[first : first + STRIP, :, chans].reshape(strip_q, group) * scale, diag
            )
            g_wide = spread(g_ref[first : first + STRIP, :, chans].reshape(strip_q, group), diag)
            at = s * (HEADS // PACK) + part
            scores = jnp.where(allowed, mm(keys, q_wide, NT), -1e30)
            probs = jnp.exp(scores - norm_ref[at : at + 1, :])
            low_probs = probs.astype(jnp.bfloat16)
            grad_prob = mm(values, g_wide, NT)
            delta = jnp.sum(low_probs.astype(jnp.float32) * grad_prob, axis=0, keepdims=True)
            grad_score = (probs * (grad_prob - delta)).astype(jnp.bfloat16)
            dq_t[chans, here] = diagonal(mm(kt[chans, window], grad_score, NN), head, strip_q) * scale
            acc[first : first + slab_rows, :, chans] += mm(grad_score, q_wide, NN).reshape(
                slab_rows, wide, group
            )
            acc[first : first + slab_rows, :, vchans] += mm(low_probs, g_wide, NN).reshape(
                slab_rows, wide, group
            )

    left_ref[...] = acc[:, cols : cols + SIDE, :].astype(jnp.bfloat16)
    right_ref[...] = acc[:, cols + SIDE : wide, :].astype(jnp.bfloat16)
    rim_ref[0:RADIUS] = acc[0:RADIUS, 0:cols, :].astype(jnp.bfloat16)
    rim_ref[RADIUS:] = acc[RADIUS + rows :, 0:cols, :].astype(jnp.bfloat16)
    mid_ref[...] = acc[RADIUS : RADIUS + rows, 0:cols, :].astype(jnp.bfloat16)
    dq_ref[...] = dq_t[...].T.astype(jnp.bfloat16).reshape(rows, cols, inner)


def share_kernel(parts_ref, copies_ref):
    total = jnp.sum(parts_ref[...].astype(jnp.float32), axis=0).astype(jnp.bfloat16)
    copies_ref[...] = jnp.broadcast_to(total[None], copies_ref.shape)


def pack_kernel(keys_ref, values_ref, both_ref, sems):
    inner = keys_ref.shape[2]
    copies = [
        pltpu.make_async_copy(keys_ref, both_ref.at[:, :, pl.ds(0, inner)], sems.at[0]),
        pltpu.make_async_copy(values_ref, both_ref.at[:, :, pl.ds(inner, inner)], sems.at[1]),
    ]
    for copy in copies:
        copy.start()
    for copy in copies:
        copy.wait()


def fold_kernel(keep_ref, got_ref, half_ref):
    half_ref[...] = (keep_ref[...] + got_ref[...].astype(jnp.float32)).astype(jnp.bfloat16)


def sum_kernel(terms_ref, out_ref):
    out_ref[...] = jnp.sum(terms_ref[...].astype(jnp.float32), axis=0).astype(jnp.bfloat16)


def mean_kernel(parts, terms_ref, out_ref):
    out_ref[...] = jnp.sum(terms_ref[...].astype(jnp.float32), axis=0) / parts


def wide(block):
    return block.astype(jnp.float32)


def rim_kernel(rim_ref, west_ref, east_ref, top_ref, bottom_ref):
    deep = top_ref.shape[0]
    for out, at, there in (
        (top_ref, 0, 0),
        (bottom_ref, deep, west_ref.shape[0] - deep),
    ):
        side = jnp.concatenate(
            [wide(west_ref[there : there + deep]), wide(east_ref[there : there + deep])], axis=1
        )
        out[...] = (wide(rim_ref[at : at + deep]) + side).astype(jnp.bfloat16)


def finish_kernel(
    mid_ref, west_ref, east_ref, above_ref, below_ref, keys_ref, values_ref
):
    inner = keys_ref.shape[2]
    deep = above_ref.shape[0]
    for out, chans in ((keys_ref, slice(0, inner)), (values_ref, slice(inner, 2 * inner))):
        for at, pole in ((0, above_ref), (deep, below_ref)):
            there = slice(deep + at, 2 * deep + at)
            side = jnp.concatenate(
                [wide(west_ref[there, :, chans]), wide(east_ref[there, :, chans])], axis=1
            )
            total = wide(mid_ref[at : at + deep, :, chans]) + side + wide(pole[:, :, chans])
            out[at : at + deep] = total.astype(jnp.bfloat16)


VMEM = pl.BlockSpec(memory_space=pltpu.VMEM)
SMEM = pl.BlockSpec(memory_space=pltpu.SMEM)
PARAMS = pltpu.CompilerParams(vmem_limit_bytes=20 << 20)
FOLD, RIM, FINISH = 1_000_000, 1_000_000, 3_000_000_000
SMALL = pltpu.CompilerParams(vmem_limit_bytes=8 << 20)


def shape(dims, kind=jnp.bfloat16):
    return jax.ShapeDtypeStruct(dims, kind)


def forward(place, queries, extended, west, east, upstream, lat_total, out_rows):
    rows, cols, inner = queries.shape
    ext_rows, wide = rows + 2 * RADIUS, cols + 2 * SIDE
    model = upstream.shape[1]
    return pl.pallas_call(
        functools.partial(forward_kernel, lat_total),
        out_shape=(
            shape((ext_rows, wide, 2 * inner)),
            shape((8, PACK * STRIP * cols), jnp.float32),
            shape((inner // (2 * out_rows), out_rows, model), jnp.float32),
            shape((inner // (2 * out_rows), out_rows, model)),
        ),
        in_specs=[SMEM] + [VMEM] * 5,
        out_specs=(VMEM,) * 4,
        scratch_shapes=[
            pltpu.VMEM((inner, ext_rows * wide), jnp.bfloat16),
            pltpu.VMEM((inner, rows * cols), jnp.float32),
        ],
        compiler_params=PARAMS,
        cost_estimate=pl.CostEstimate(
            flops=1_000_000_000, bytes_accessed=5_000_000, transcendentals=800_000
        ),
        name="forward",
    )(place, queries, extended, west, east, upstream)


def backward(place, queries, grads, kv, norm, lat_total):
    rows, cols, inner = queries.shape
    ext_rows, wide = rows + 2 * RADIUS, cols + 2 * SIDE
    return pl.pallas_call(
        functools.partial(backward_kernel, lat_total),
        out_shape=(
            shape((rows, cols, inner)),
            shape((rows, cols, 2 * inner)),
            shape((2 * RADIUS, cols, 2 * inner)),
            shape((ext_rows, SIDE, 2 * inner)),
            shape((ext_rows, SIDE, 2 * inner)),
        ),
        in_specs=[SMEM] + [VMEM] * 4,
        out_specs=(VMEM,) * 5,
        scratch_shapes=[
            pltpu.VMEM((inner, ext_rows * wide), jnp.bfloat16),
            pltpu.VMEM((ext_rows, wide, 2 * inner), jnp.float32),
            pltpu.VMEM((inner, rows * cols), jnp.float32),
        ],
        compiler_params=PARAMS,
        cost_estimate=pl.CostEstimate(
            flops=20_000_000_000, bytes_accessed=70_000_000, transcendentals=800_000
        ),
        name="backward",
    )(place, queries, grads, kv, norm)


def ring(block, axis, by):
    size = lax.axis_size(axis)
    return lax.ppermute(block, axis, [(i, (i + by) % size) for i in range(size)])


def line(block, axis, by):
    size = lax.axis_size(axis)
    return lax.ppermute(
        block, axis, [(i, i + by) for i in range(size) if 0 <= i + by < size]
    )


def cost(flops):
    return pl.CostEstimate(flops=flops, bytes_accessed=4_000_000, transcendentals=0)


def shards(queries, keys, values, upstream, out_weight):
    rows, cols, inner = queries.shape
    model = upstream.shape[2]
    tokens = rows * cols
    lat, lon = lax.axis_size("lat"), lax.axis_size("lon")
    lat_total = rows * lat
    out_rows = inner // lon
    place = jnp.stack([lax.axis_index("lat") * rows, lax.axis_index("lon") % 2]).astype(jnp.int32)
    up_flat = upstream.reshape(tokens, model)
    grads = (
        jnp.einsum("td,id->ti", up_flat, out_weight, preferred_element_type=jnp.float32)
        .astype(jnp.bfloat16)
        .reshape(rows, cols, inner)
    )
    both = pl.pallas_call(
        pack_kernel,
        out_shape=shape((rows, cols, 2 * inner)),
        in_specs=[pl.BlockSpec(memory_space=pl.ANY)] * 2,
        out_specs=VMEM,
        scratch_shapes=[pltpu.SemaphoreType.DMA((2,))],
        compiler_params=SMALL,
        name="pack",
    )(keys, values)
    above = line(both[rows - RADIUS :], "lat", 1)
    below = line(both[:RADIUS], "lat", -1)
    extended = jnp.concatenate([above, both, below], axis=0)
    west = ring(extended[:, cols - SIDE :], "lon", 1)
    east = ring(extended[:, :SIDE], "lon", -1)
    place, grads = lax.optimization_barrier((place, grads))
    kv, norm, keep, give = forward(
        place, queries, extended, west, east, up_flat, lat_total, out_rows
    )
    got = lax.ppermute(give, "lon", [(i, i ^ 1) for i in range(lon)])
    grad_query, mid, rim, left, right = backward(
        place, queries, grads, kv, norm, lat_total
    )
    keep, left, right = lax.optimization_barrier((keep, left, right))
    from_east = ring(left, "lon", -1)
    from_west = ring(right, "lon", 1)
    half = pl.pallas_call(
        fold_kernel,
        out_shape=shape(keep.shape),
        compiler_params=SMALL,
        cost_estimate=cost(FOLD),
        name="fold",
    )(keep, got)
    near, step = 4, 8
    far = lon // step
    far_groups = [[j + step * i for i in range(far)] for j in range(step)]
    near_groups = [
        [step * f + 2 * n + c for n in range(near)] for f in range(far) for c in range(2)
    ]
    spread_far = lax.all_to_all(
        half.reshape(far, near * out_rows, model), "lon", 0, 0, axis_index_groups=far_groups, tiled=True
    )
    rim, _ = lax.optimization_barrier((rim, half))
    top, bottom = pl.pallas_call(
        rim_kernel,
        out_shape=(shape((RADIUS, cols, 2 * inner)),) * 2,
        compiler_params=SMALL,
        cost_estimate=cost(RIM),
        name="rim",
    )(rim, from_west, from_east)
    spread_far, _ = lax.optimization_barrier((spread_far, top))
    quarter = pl.pallas_call(
        sum_kernel,
        out_shape=shape((near * out_rows, model)),
        compiler_params=SMALL,
        name="sum_far",
    )(spread_far)
    terms = lax.all_to_all(
        quarter.reshape(near, out_rows, model), "lon", 0, 0, axis_index_groups=near_groups, tiled=True
    )
    top, bottom, terms = lax.optimization_barrier((top, bottom, terms))
    from_below = line(top, "lat", -1)
    from_above = line(bottom, "lat", 1)
    copies = pl.pallas_call(
        share_kernel,
        out_shape=shape((lat, out_rows, model)),
        compiler_params=SMALL,
        name="share",
    )(terms)
    every = lax.all_to_all(copies, "lat", 0, 0, tiled=True)
    mid, _ = lax.optimization_barrier((mid, copies))
    grad_key, grad_value = pl.pallas_call(
        finish_kernel,
        out_shape=(shape((rows, cols, inner)),) * 2,
        compiler_params=SMALL,
        cost_estimate=cost(FINISH),
        name="finish",
    )(mid, from_west, from_east, from_above, from_below)
    grad_weight = pl.pallas_call(
        functools.partial(mean_kernel, lat_total),
        out_shape=shape((out_rows, model), jnp.float32),
        compiler_params=SMALL,
        name="mean",
    )(every)
    return (grad_query, grad_key, grad_value, grad_weight)


def solution(mesh):
    placed = P("lat", "lon", None)
    return jax.shard_map(
        shards,
        mesh=mesh,
        in_specs=(placed, placed, placed, placed, P()),
        out_specs=(placed, placed, placed, P("lon", None)),
        check_vma=False,
    )
```

```python
import functools

import jax
import jax.numpy as jnp
from jax import lax
from jax.experimental import pallas as pl
from jax.experimental.pallas import tpu as pltpu
from jax.sharding import PartitionSpec as P

HEADS = 8
RADIUS = 6
SIDE = 8
STRIP = 4
PACK = 4

NT = (((1,), (1,)), ((), ()))
NN = (((1,), (0,)), ((), ()))


def mm(a, b, dims):
    return lax.dot_general(a, b, dims, preferred_element_type=jnp.float32)


def spread(block, diag):
    tall = jnp.concatenate([block.astype(jnp.float32)] * PACK, axis=0)
    return jnp.where(diag, tall, 0.0).astype(jnp.bfloat16)


def diagonal(square, head, strip_q):
    return jnp.concatenate(
        [square[h * head : (h + 1) * head, h * strip_q : (h + 1) * strip_q] for h in range(PACK)],
        axis=0,
    )


def masks(rows, cols, inner):
    head = inner // HEADS
    wide = cols + 2 * SIDE
    strip_q = STRIP * cols
    slab = (STRIP + 2 * RADIUS) * wide
    lanes = PACK * strip_q
    key = lax.broadcasted_iota(jnp.int32, (slab, lanes), 0)
    query = lax.broadcasted_iota(jnp.int32, (slab, lanes), 1) & (strip_q - 1)
    row = key // wide
    place = key & (wide - 1)
    col = jnp.where(
        place < cols, place, jnp.where(place < cols + SIDE, place - cols - SIDE, place - SIDE)
    )
    row_gap = row - query // cols
    col_gap = jnp.abs(col - (query & (cols - 1)))
    near = (row_gap >= 0) & (row_gap <= 2 * RADIUS) & (col_gap <= RADIUS)
    diag = (lax.broadcasted_iota(jnp.int32, (lanes, PACK * head), 0) // strip_q) == (
        lax.broadcasted_iota(jnp.int32, (lanes, PACK * head), 1) // head
    )
    return near, row, diag


def forward_kernel(
    lat_total, place_ref, q_ref, ext_ref, west_ref, east_ref, up_ref,
    kv_ref, norm_ref, keep_ref, give_ref, vt, att_t,
):
    rows, cols, inner = q_ref.shape
    ext_rows = rows + 2 * RADIUS
    wide = cols + 2 * SIDE
    head = inner // HEADS
    scale = head ** (-0.5)
    group = PACK * head
    strip_q = STRIP * cols
    slab_rows = STRIP + 2 * RADIUS
    slab = slab_rows * wide
    base, core = place_ref[0], place_ref[1]

    kv_ref[:, 0:cols, :] = ext_ref[...]
    kv_ref[:, cols:wide, :] = jnp.concatenate(
        [west_ref[...].astype(jnp.float32), east_ref[...].astype(jnp.float32)], axis=1
    ).astype(jnp.bfloat16)
    vt[...] = kv_ref[:, :, inner:].reshape(ext_rows * wide, inner).T
    near, row, diag = masks(rows, cols, inner)

    for s in range(rows // STRIP):
        first = s * STRIP
        low = RADIUS - base - first
        allowed = near & (row >= low) & (row < low + lat_total)
        window = slice(first * wide, first * wide + slab)
        here = slice(s * strip_q, (s + 1) * strip_q)
        for part in range(HEADS // PACK):
            chans = slice(part * group, (part + 1) * group)
            keys = kv_ref[first : first + slab_rows, :, chans].reshape(slab, group)
            q_wide = spread(
                q_ref[first : first + STRIP, :, chans].reshape(strip_q, group) * scale, diag
            )
            scores = jnp.where(allowed, mm(keys, q_wide, NT), -1e30)
            top = jnp.max(scores, axis=0, keepdims=True)
            weights = jnp.exp(scores - top)
            total = jnp.sum(weights, axis=0, keepdims=True)
            probs = (weights * (1.0 / total)).astype(jnp.bfloat16)
            at = s * (HEADS // PACK) + part
            norm_ref[at : at + 1, :] = top + jnp.log(total)
            att_t[chans, here] = diagonal(mm(vt[chans, window], probs, NN), head, strip_q)

    weight = mm(att_t[...].astype(jnp.bfloat16), up_ref[...], NN)
    out_rows = keep_ref.shape[1]
    weight = weight.reshape(keep_ref.shape[0], 2, out_rows, weight.shape[1])
    keep_ref[...] = jnp.where(core == 0, weight[:, 0], weight[:, 1])
    give_ref[...] = jnp.where(core == 0, weight[:, 1], weight[:, 0]).astype(jnp.bfloat16)


def backward_kernel(
    lat_total, place_ref, q_ref, g_ref, kv_ref, norm_ref,
    dq_ref, mid_ref, rim_ref, left_ref, right_ref, kt, acc, dq_t,
):
    rows, cols, inner = q_ref.shape
    ext_rows = rows + 2 * RADIUS
    wide = cols + 2 * SIDE
    head = inner // HEADS
    scale = head ** (-0.5)
    group = PACK * head
    strip_q = STRIP * cols
    slab_rows = STRIP + 2 * RADIUS
    slab = slab_rows * wide
    base = place_ref[0]

    kt[...] = kv_ref[:, :, 0:inner].reshape(ext_rows * wide, inner).T
    acc[...] = jnp.zeros_like(acc)
    near, row, diag = masks(rows, cols, inner)

    for s in range(rows // STRIP):
        first = s * STRIP
        low = RADIUS - base - first
        allowed = near & (row >= low) & (row < low + lat_total)
        window = slice(first * wide, first * wide + slab)
        here = slice(s * strip_q, (s + 1) * strip_q)
        for part in range(HEADS // PACK):
            chans = slice(part * group, (part + 1) * group)
            vchans = slice(inner + part * group, inner + (part + 1) * group)
            keys = kv_ref[first : first + slab_rows, :, chans].reshape(slab, group)
            values = kv_ref[first : first + slab_rows, :, vchans].reshape(slab, group)
            q_wide = spread(
                q_ref[first : first + STRIP, :, chans].reshape(strip_q, group) * scale, diag
            )
            g_wide = spread(g_ref[first : first + STRIP, :, chans].reshape(strip_q, group), diag)
            at = s * (HEADS // PACK) + part
            scores = jnp.where(allowed, mm(keys, q_wide, NT), -1e30)
            probs = jnp.exp(scores - norm_ref[at : at + 1, :])
            low_probs = probs.astype(jnp.bfloat16)
            grad_prob = mm(values, g_wide, NT)
            delta = jnp.sum(low_probs.astype(jnp.float32) * grad_prob, axis=0, keepdims=True)
            grad_score = (probs * (grad_prob - delta)).astype(jnp.bfloat16)
            dq_t[chans, here] = diagonal(mm(kt[chans, window], grad_score, NN), head, strip_q) * scale
            acc[first : first + slab_rows, :, chans] += mm(grad_score, q_wide, NN).reshape(
                slab_rows, wide, group
            )
            acc[first : first + slab_rows, :, vchans] += mm(low_probs, g_wide, NN).reshape(
                slab_rows, wide, group
            )

    left_ref[...] = acc[:, cols : cols + SIDE, :].astype(jnp.bfloat16)
    right_ref[...] = acc[:, cols + SIDE : wide, :].astype(jnp.bfloat16)
    rim_ref[0:RADIUS] = acc[0:RADIUS, 0:cols, :].astype(jnp.bfloat16)
    rim_ref[RADIUS:] = acc[RADIUS + rows :, 0:cols, :].astype(jnp.bfloat16)
    mid_ref[...] = acc[RADIUS : RADIUS + rows, 0:cols, :].astype(jnp.bfloat16)
    dq_ref[...] = dq_t[...].T.astype(jnp.bfloat16).reshape(rows, cols, inner)


def share_kernel(parts_ref, copies_ref):
    total = jnp.sum(parts_ref[...].astype(jnp.float32), axis=0).astype(jnp.bfloat16)
    copies_ref[...] = jnp.broadcast_to(total[None], copies_ref.shape)


def pack_kernel(keys_ref, values_ref, both_ref, sems):
    inner = keys_ref.shape[2]
    copies = [
        pltpu.make_async_copy(keys_ref, both_ref.at[:, :, pl.ds(0, inner)], sems.at[0]),
        pltpu.make_async_copy(values_ref, both_ref.at[:, :, pl.ds(inner, inner)], sems.at[1]),
    ]
    for copy in copies:
        copy.start()
    for copy in copies:
        copy.wait()


def edge_kernel(above_ref, both_ref, below_ref, ext_ref, last_ref, first_ref):
    deep, rows = above_ref.shape[0], both_ref.shape[0]
    cols = both_ref.shape[1]
    for at, size, source in (
        (0, deep, above_ref),
        (deep, rows, both_ref),
        (deep + rows, deep, below_ref),
    ):
        ext_ref[at : at + size] = source[...]
        block = source[...].astype(jnp.float32)
        first_ref[at : at + size] = block[:, :SIDE].astype(jnp.bfloat16)
        last_ref[at : at + size] = block[:, cols - SIDE :].astype(jnp.bfloat16)


def fold_kernel(keep_ref, got_ref, half_ref):
    half_ref[...] = (keep_ref[...] + got_ref[...].astype(jnp.float32)).astype(jnp.bfloat16)


def mean_kernel(parts, terms_ref, out_ref):
    out_ref[...] = jnp.sum(terms_ref[...].astype(jnp.float32), axis=0) / parts


def wide(block):
    return block.astype(jnp.float32)


def rim_kernel(rim_ref, west_ref, east_ref, top_ref, bottom_ref):
    deep = top_ref.shape[0]
    for out, at, there in (
        (top_ref, 0, 0),
        (bottom_ref, deep, west_ref.shape[0] - deep),
    ):
        side = jnp.concatenate(
            [wide(west_ref[there : there + deep]), wide(east_ref[there : there + deep])], axis=1
        )
        out[...] = (wide(rim_ref[at : at + deep]) + side).astype(jnp.bfloat16)


def finish_kernel(
    mid_ref, west_ref, east_ref, above_ref, below_ref, keys_ref, values_ref
):
    inner = keys_ref.shape[2]
    deep = above_ref.shape[0]
    for out, chans in ((keys_ref, slice(0, inner)), (values_ref, slice(inner, 2 * inner))):
        for at, pole in ((0, above_ref), (deep, below_ref)):
            there = slice(deep + at, 2 * deep + at)
            side = jnp.concatenate(
                [wide(west_ref[there, :, chans]), wide(east_ref[there, :, chans])], axis=1
            )
            total = wide(mid_ref[at : at + deep, :, chans]) + side + wide(pole[:, :, chans])
            out[at : at + deep] = total.astype(jnp.bfloat16)


VMEM = pl.BlockSpec(memory_space=pltpu.VMEM)
SMEM = pl.BlockSpec(memory_space=pltpu.SMEM)
PARAMS = pltpu.CompilerParams(vmem_limit_bytes=20 << 20)
FOLD, RIM, FINISH = 1_000_000, 1_000_000, 3_000_000_000
SMALL = pltpu.CompilerParams(vmem_limit_bytes=8 << 20)


def shape(dims, kind=jnp.bfloat16):
    return jax.ShapeDtypeStruct(dims, kind)


def forward(place, queries, extended, west, east, upstream, lat_total, out_rows):
    rows, cols, inner = queries.shape
    ext_rows, wide = rows + 2 * RADIUS, cols + 2 * SIDE
    model = upstream.shape[1]
    return pl.pallas_call(
        functools.partial(forward_kernel, lat_total),
        out_shape=(
            shape((ext_rows, wide, 2 * inner)),
            shape((8, PACK * STRIP * cols), jnp.float32),
            shape((inner // (2 * out_rows), out_rows, model), jnp.float32),
            shape((inner // (2 * out_rows), out_rows, model)),
        ),
        in_specs=[SMEM] + [VMEM] * 5,
        out_specs=(VMEM,) * 4,
        scratch_shapes=[
            pltpu.VMEM((inner, ext_rows * wide), jnp.bfloat16),
            pltpu.VMEM((inner, rows * cols), jnp.float32),
        ],
        compiler_params=PARAMS,
        cost_estimate=pl.CostEstimate(
            flops=1_000_000_000, bytes_accessed=5_000_000, transcendentals=800_000
        ),
        name="forward",
    )(place, queries, extended, west, east, upstream)


def backward(place, queries, grads, kv, norm, lat_total):
    rows, cols, inner = queries.shape
    ext_rows, wide = rows + 2 * RADIUS, cols + 2 * SIDE
    return pl.pallas_call(
        functools.partial(backward_kernel, lat_total),
        out_shape=(
            shape((rows, cols, inner)),
            shape((rows, cols, 2 * inner)),
            shape((2 * RADIUS, cols, 2 * inner)),
            shape((ext_rows, SIDE, 2 * inner)),
            shape((ext_rows, SIDE, 2 * inner)),
        ),
        in_specs=[SMEM] + [VMEM] * 4,
        out_specs=(VMEM,) * 5,
        scratch_shapes=[
            pltpu.VMEM((inner, ext_rows * wide), jnp.bfloat16),
            pltpu.VMEM((ext_rows, wide, 2 * inner), jnp.float32),
            pltpu.VMEM((inner, rows * cols), jnp.float32),
        ],
        compiler_params=PARAMS,
        cost_estimate=pl.CostEstimate(
            flops=20_000_000_000, bytes_accessed=70_000_000, transcendentals=800_000
        ),
        name="backward",
    )(place, queries, grads, kv, norm)


def ring(block, axis, by):
    size = lax.axis_size(axis)
    return lax.ppermute(block, axis, [(i, (i + by) % size) for i in range(size)])


def line(block, axis, by):
    size = lax.axis_size(axis)
    return lax.ppermute(
        block, axis, [(i, i + by) for i in range(size) if 0 <= i + by < size]
    )


def cost(flops):
    return pl.CostEstimate(flops=flops, bytes_accessed=4_000_000, transcendentals=0)


def shards(queries, keys, values, upstream, out_weight):
    rows, cols, inner = queries.shape
    model = upstream.shape[2]
    tokens = rows * cols
    lat, lon = lax.axis_size("lat"), lax.axis_size("lon")
    lat_total = rows * lat
    out_rows = inner // lon
    place = jnp.stack([lax.axis_index("lat") * rows, lax.axis_index("lon") % 2]).astype(jnp.int32)
    up_flat = upstream.reshape(tokens, model)
    grads = (
        jnp.einsum("td,id->ti", up_flat, out_weight, preferred_element_type=jnp.float32)
        .astype(jnp.bfloat16)
        .reshape(rows, cols, inner)
    )
    both = pl.pallas_call(
        pack_kernel,
        out_shape=shape((rows, cols, 2 * inner)),
        in_specs=[pl.BlockSpec(memory_space=pltpu.HBM)] * 2,
        out_specs=VMEM,
        scratch_shapes=[pltpu.SemaphoreType.DMA((2,))],
        compiler_params=SMALL,
        name="pack",
    )(keys, values)
    above = line(both[rows - RADIUS :], "lat", 1)
    below = line(both[:RADIUS], "lat", -1)
    ext_rows = rows + 2 * RADIUS
    extended, last, first = pl.pallas_call(
        edge_kernel,
        out_shape=(
            shape((ext_rows, cols, 2 * inner)),
            shape((ext_rows, SIDE, 2 * inner)),
            shape((ext_rows, SIDE, 2 * inner)),
        ),
        compiler_params=SMALL,
        name="edge",
    )(above, both, below)
    west = ring(last, "lon", 1)
    east = ring(first, "lon", -1)
    place, grads = lax.optimization_barrier((place, grads))
    kv, norm, keep, give = forward(
        place, queries, extended, west, east, up_flat, lat_total, out_rows
    )
    got = lax.ppermute(give, "lon", [(i, i ^ 1) for i in range(lon)])
    half = pl.pallas_call(
        fold_kernel,
        out_shape=shape(keep.shape),
        compiler_params=SMALL,
        cost_estimate=cost(FOLD),
        name="fold",
    )(keep, got)
    same_core = [[2 * i + c for i in range(lon // 2)] for c in range(2)]
    terms = lax.all_to_all(half, "lon", 0, 0, axis_index_groups=same_core, tiled=True)
    after, _ = lax.optimization_barrier((place, half))
    grad_query, mid, rim, left, right = backward(
        after, queries, grads, kv, norm, lat_total
    )
    from_east = ring(left, "lon", -1)
    from_west = ring(right, "lon", 1)
    top, bottom = pl.pallas_call(
        rim_kernel,
        out_shape=(shape((RADIUS, cols, 2 * inner)),) * 2,
        compiler_params=SMALL,
        cost_estimate=cost(RIM),
        name="rim",
    )(rim, from_west, from_east)
    from_below = line(top, "lat", -1)
    from_above = line(bottom, "lat", 1)
    terms, _ = lax.optimization_barrier((terms, top))
    copies = pl.pallas_call(
        share_kernel,
        out_shape=shape((lat, out_rows, model)),
        compiler_params=SMALL,
        name="share",
    )(terms)
    every = lax.all_to_all(copies, "lat", 0, 0, tiled=True)
    mid, _ = lax.optimization_barrier((mid, copies))
    grad_key, grad_value = pl.pallas_call(
        finish_kernel,
        out_shape=(shape((rows, cols, inner)),) * 2,
        compiler_params=SMALL,
        cost_estimate=cost(FINISH),
        name="finish",
    )(mid, from_west, from_east, from_above, from_below)
    grad_weight = pl.pallas_call(
        functools.partial(mean_kernel, lat_total),
        out_shape=shape((out_rows, model), jnp.float32),
        compiler_params=SMALL,
        name="mean",
    )(every)
    return (grad_query, grad_key, grad_value, grad_weight)


def solution(mesh):
    placed = P("lat", "lon", None)
    return jax.shard_map(
        shards,
        mesh=mesh,
        in_specs=(placed, placed, placed, placed, P()),
        out_specs=(placed, placed, placed, P("lon", None)),
        check_vma=False,
    )
```
